256 devices in a mesh: dp: 32 (over x, y, core), mp: 8 (over z).
Axes of the slice: x: 4, y: 4, z: 8, core: 2. Of those that a mesh axis runs over, the one named last changes fastest.
Arguments:
- patches: bfloat16 [16384, 6144], P('dp', 'mp'), may hold values from -200 to 200
- norm_gain: float32 [6144], replicated, may hold values from 0.25 to 1.75
- value_weight: bfloat16 [6144, 3072], P(None, 'mp'), may hold values from -0.078125 to 0.078125
- queries: bfloat16 [16384, 3072], P('dp', 'mp'), may hold values from -100 to 100
- key_vectors: bfloat16 [16384, 3072], P('dp', 'mp'), may hold values from -4 to 4
- head_cotangent: bfloat16 [32768, 3072], P('dp', 'mp'), may hold values from -6 to 6
- image_owner: int32 [32, 32], replicated, may hold values from 0 to 31, as said below
- patch_count: int32 [32, 32], replicated, may hold values from 0 to 32, as said below
Outputs:
- value_grad: float32 [6144, 3072], P('dp', 'mp')
- query_grad: bfloat16 [16384, 3072], P('dp', 'mp')
- key_grad: bfloat16 [16384, 3072], P('dp', 'mp')
The draws below stay inside these ranges and needn't reach their ends.
Inputs may be any that keep to these rules, and one draw needn't show every extreme that they name: `image_owner`: each row lists every owner once. `patch_count`: 0 marks an empty image slot; each row sums to 512; some owner receives 32 patches from every device.
All inputs are finite; a program needn't handle non-finite values.
Results may differ from the reference program's by a relative error of at most 0.0065.
Values may be sent and summed in bfloat16 or wider, within the bound.
A program may use at most 128 MiB of HBM per device.

```python
import math
import jax
import jax.numpy as jnp
from jax import lax

D = 6144
HEADS = 24
HD = 128
CAP = 32
ROWS_DEV = 512
SLOTS = 1024
TOTAL_ROWS = 16384
N_DP = 32


def plan_tables(key):
    key_special = jax.random.fold_in(key, 101)
    key_portion = jax.random.fold_in(key, 102)
    key_order = jax.random.fold_in(key, 103)
    special = jax.random.randint(key_special, (), 0, N_DP)
    portion = jax.random.randint(key_portion, (N_DP, N_DP // 2), 0, CAP + 1)
    column = jnp.arange(N_DP // 2, dtype=jnp.int32)
    forced = jnp.where(special % 2 == 0, CAP, 0)
    portion = jnp.where(column[None, :] == special // 2, forced, portion)
    to_owner = jnp.stack([portion, CAP - portion], axis=2).reshape(N_DP, N_DP)
    order_keys = jax.random.split(key_order, N_DP)
    owners = jax.vmap(lambda single: jax.random.permutation(single, N_DP))(order_keys).astype(jnp.int32)
    counts = jnp.take_along_axis(to_owner, owners, axis=1).astype(jnp.int32)
    return (owners, counts)


def draw_image_owner(key, part):
    return plan_tables(key)[0]


def draw_patch_count(key, part):
    return plan_tables(key)[1]


def draw_patches(key, part):
    column_scale = jnp.exp(jax.random.uniform(jax.random.fold_in(key, 202), (D,), minval=math.log(0.5), maxval=math.log(5.0)))
    base = jnp.clip(jax.random.normal(jax.random.fold_in(key, 201), (TOTAL_ROWS, D)), -4.0, 4.0)
    row_scale = jnp.exp(jax.random.uniform(jax.random.fold_in(key, 203), (TOTAL_ROWS,), minval=math.log(0.5), maxval=math.log(5.0)))
    return (base * column_scale[None, :] * row_scale[:, None]).astype(jnp.bfloat16)


def query_key(key):
    key_part = jnp.clip(jax.random.normal(jax.random.fold_in(key, 301), (TOTAL_ROWS, HEADS * HD)), -4.0, 4.0)
    query_part = jnp.clip(jax.random.normal(jax.random.fold_in(key, 302), (TOTAL_ROWS, HEADS * HD)), -4.0, 4.0)
    return (query_part.astype(jnp.float32), key_part.astype(jnp.float32))


def draw_queries(key, part):
    return query_key(key)[0].astype(jnp.bfloat16)


def draw_key_vectors(key, part):
    return query_key(key)[1].astype(jnp.bfloat16)


def block_levels(stream_key, dims, cuts, low, top_value):
    def one(dim, blocks):
        steps = jax.random.uniform(jax.random.fold_in(jax.random.fold_in(stream_key, 6), dim), (blocks,), jnp.float32, low / len(cuts), top_value / len(cuts))
        return jnp.repeat(jnp.exp(steps), dims[dim] // blocks).reshape((-1,) + (1,) * (len(dims) - dim - 1))

    level = one(*cuts[0])
    for cut in cuts[1:]:
        level = level * one(*cut)
    return level


def noise(stream_key, dims, scale, reach, shards=(), kind=jnp.bfloat16):
    loudness = block_levels(stream_key, dims, shards, -0.22, 0.18) if shards else 1.0
    result = jax.random.normal(stream_key, dims, jnp.float32) * scale * loudness
    return jnp.minimum(jnp.maximum(result, -reach), reach).astype(kind)


def setup_inputs(seed: int = 0) -> dict:
    seeds = jax.random.split(jax.random.key(seed), 9)
    patches = draw_patches(jax.random.fold_in(seeds[8], 71), 0)
    norm_gain = jnp.clip(1.0 + 0.15 * jax.random.normal(seeds[1], (D,), jnp.float32), 0.25, 1.75)
    value_weight = noise(seeds[2], (D, HEADS * HD), D ** -0.5, 0.078125, ((1, 8),))
    queries = draw_queries(jax.random.fold_in(seeds[8], 71), 0)
    key_vectors = draw_key_vectors(jax.random.fold_in(seeds[8], 71), 0)
    head_cotangent = noise(seeds[5], (N_DP * SLOTS, HEADS * HD), 1.0, 6.0, ((0, 32), (1, 8)))
    image_owner = draw_image_owner(jax.random.fold_in(seeds[8], 71), 0)
    patch_count = draw_patch_count(jax.random.fold_in(seeds[8], 71), 0)
    return {"patches": patches, "norm_gain": norm_gain, "value_weight": value_weight, "queries": queries, "key_vectors": key_vectors, "head_cotangent": head_cotangent, "image_owner": image_owner, "patch_count": patch_count}


def normalize(rows, norm_gain):
    values = rows.astype(jnp.float32)
    average = lax.optimization_barrier(jnp.mean(values, axis=-1, keepdims=True))
    centred = values - average
    variance = lax.optimization_barrier(jnp.mean(centred * centred, axis=-1, keepdims=True))
    return (centred * lax.rsqrt(variance + 1e-06) * norm_gain).astype(jnp.bfloat16)

def attention_grads(query_rows, key_rows, value_rows, cotangent, segment):
    total = query_rows.shape[0]
    heads_here = query_rows.shape[1] // HD
    scale = HD ** (-0.5)
    query_heads = query_rows.reshape(total, heads_here, HD).astype(jnp.float32)
    key_heads = key_rows.reshape(total, heads_here, HD).astype(jnp.float32)
    value_heads = value_rows.reshape(total, heads_here, HD).astype(jnp.float32)
    cot_heads = cotangent.reshape(total, heads_here, HD).astype(jnp.float32)
    scores = jnp.einsum('qhd,khd->hqk', query_heads, key_heads) * scale
    allowed = segment[:, None] == segment[None, :]
    scores = jnp.where(allowed[None], scores, -1000000000.0)
    peak = lax.optimization_barrier(jnp.max(scores, axis=-1, keepdims=True))
    weights = jnp.exp(scores - peak)
    weights = weights / lax.optimization_barrier(jnp.sum(weights, axis=-1, keepdims=True))
    rounded = weights.astype(jnp.bfloat16).astype(jnp.float32)
    value_grad = jnp.einsum('hqk,qhd->khd', rounded, cot_heads).astype(jnp.bfloat16)
    prob_grad = jnp.einsum('qhd,khd->hqk', cot_heads, value_heads)
    centre = lax.optimization_barrier(jnp.sum(weights * prob_grad, axis=-1, keepdims=True))
    score_grad = (weights * (prob_grad - centre)).astype(jnp.bfloat16).astype(jnp.float32)
    query_grad = (jnp.einsum('hqk,khd->qhd', score_grad, key_heads) * scale).astype(jnp.bfloat16)
    key_grad = (jnp.einsum('hqk,qhd->khd', score_grad, query_heads) * scale).astype(jnp.bfloat16)
    width = heads_here * HD
    return (value_grad.reshape(total, width), query_grad.reshape(total, width), key_grad.reshape(total, width))

def reference(patches, norm_gain, value_weight, queries, key_vectors, head_cotangent, image_owner, patch_count):

    def one_source(source):
        first = (source * ROWS_DEV).astype(jnp.int32)
        rows = lax.dynamic_slice_in_dim(patches, first, ROWS_DEV, 0)
        query_rows = lax.dynamic_slice_in_dim(queries, first, ROWS_DEV, 0)
        key_rows = lax.dynamic_slice_in_dim(key_vectors, first, ROWS_DEV, 0)
        own_list = lax.dynamic_index_in_dim(image_owner, source, 0, keepdims=False).astype(jnp.int32)
        own_count = lax.dynamic_index_in_dim(patch_count, source, 0, keepdims=False).astype(jnp.int32)
        ends = jnp.cumsum(own_count).astype(jnp.int32)
        starts = (ends - own_count).astype(jnp.int32)
        row_index = jnp.arange(ROWS_DEV, dtype=jnp.int32)
        image_of = lax.optimization_barrier(jnp.sum((ends[None, :] <= row_index[:, None]).astype(jnp.int32), axis=1)).astype(jnp.int32)
        picked = image_of[:, None] == jnp.arange(N_DP, dtype=jnp.int32)[None, :]
        row_owner = lax.optimization_barrier(jnp.sum(jnp.where(picked, own_list[None, :], 0), axis=1)).astype(jnp.int32)
        row_start = lax.optimization_barrier(jnp.sum(jnp.where(picked, starts[None, :], 0), axis=1)).astype(jnp.int32)
        packed_index = (row_owner * SLOTS + source * CAP + row_index - row_start).astype(jnp.int32)
        cotangent = head_cotangent[packed_index]
        normed = normalize(rows, norm_gain)
        value_rows = jnp.dot(normed, value_weight, preferred_element_type=jnp.float32).astype(jnp.bfloat16)
        value_grad, query_grad, key_grad = attention_grads(query_rows, key_rows, value_rows, cotangent, image_of)
        return (normed, value_grad, query_grad, key_grad)
    normed, value_rows, query_grad, key_grad = lax.map(one_source, jnp.arange(N_DP, dtype=jnp.int32))
    normed = normed.reshape(TOTAL_ROWS, D)
    value_rows = value_rows.reshape(TOTAL_ROWS, HEADS * HD)
    weight_grad = jnp.dot(normed.T, value_rows, preferred_element_type=jnp.float32)
    return (weight_grad, query_grad.reshape(TOTAL_ROWS, HEADS * HD), key_grad.reshape(TOTAL_ROWS, HEADS * HD))
```

```python
import jax
import jax.numpy as jnp
from jax import lax
from jax.sharding import PartitionSpec as P

HD = 128


def normalize(rows, norm_gain):
    values = rows.astype(jnp.float32)
    average = jnp.mean(values, axis=-1, keepdims=True)
    centred = values - average
    variance = jnp.mean(centred * centred, axis=-1, keepdims=True)
    return (centred * lax.rsqrt(variance + 1e-06) * norm_gain).astype(jnp.bfloat16)


def plan(image_owner, patch_count, rows_here, capacity):
    device = lax.axis_index("dp")
    own_list = lax.dynamic_index_in_dim(image_owner, device, 0, keepdims=False)
    own_count = lax.dynamic_index_in_dim(patch_count, device, 0, keepdims=False)
    images = own_list.shape[0]
    ends = jnp.cumsum(own_count)
    starts = ends - own_count
    row_index = jnp.arange(rows_here, dtype=jnp.int32)
    image_of = jnp.sum((ends[None, :] <= row_index[:, None]).astype(jnp.int32), axis=1)
    picked = image_of[:, None] == jnp.arange(images, dtype=jnp.int32)[None, :]
    row_owner = jnp.sum(jnp.where(picked, own_list[None, :], 0), axis=1)
    row_start = jnp.sum(jnp.where(picked, starts[None, :], 0), axis=1)
    return image_of, row_owner * capacity + row_index - row_start


def body(
    patches, norm_gain, value_weight, queries, key_vectors, head_cotangent, image_owner, patch_count
):
    devices = lax.axis_size("dp")
    rows, width = queries.shape
    heads = width // HD
    capacity = head_cotangent.shape[0] // devices
    scale = HD ** (-0.5)
    whole = lax.all_gather(patches, "mp", axis=1, tiled=True)
    image_of, index = plan(image_owner, patch_count, rows, capacity)
    packed = lax.all_to_all(
        head_cotangent.reshape(devices, capacity, width), "dp", split_axis=0, concat_axis=0, tiled=True
    ).reshape(devices * capacity, width)
    cot = packed[index].reshape(rows, heads, HD)
    q = queries.reshape(rows, heads, HD)
    k = key_vectors.reshape(rows, heads, HD)
    f32 = jnp.float32
    scores = jnp.einsum("qhd,khd->hqk", q, k, preferred_element_type=f32) * scale
    allowed = image_of[:, None] == image_of[None, :]
    scores = jnp.where(allowed[None], scores, -1e9)
    weights = jnp.exp(scores - jnp.max(scores, axis=-1, keepdims=True))
    weights = weights / jnp.sum(weights, axis=-1, keepdims=True)
    value_rows = jnp.einsum(
        "hqk,qhd->khd", weights.astype(jnp.bfloat16), cot, preferred_element_type=f32
    ).astype(jnp.bfloat16).reshape(rows, width)
    normed = normalize(whole, norm_gain)
    weight_grad = lax.psum_scatter(
        lax.dot_general(normed, value_rows, (((0,), (0,)), ((), ())), preferred_element_type=f32),
        "dp", scatter_dimension=0, tiled=True,
    )
    values = jnp.dot(normed, value_weight, preferred_element_type=f32).astype(jnp.bfloat16)
    prob_grad = jnp.einsum("qhd,khd->hqk", cot, values.reshape(rows, heads, HD), preferred_element_type=f32)
    centre = jnp.sum(weights * prob_grad, axis=-1, keepdims=True)
    score_grad = (weights * (prob_grad - centre)).astype(jnp.bfloat16)
    query_grad = jnp.einsum("hqk,khd->qhd", score_grad, k, preferred_element_type=f32) * scale
    key_grad = jnp.einsum("hqk,qhd->khd", score_grad, q, preferred_element_type=f32) * scale
    return (
        weight_grad,
        query_grad.astype(jnp.bfloat16).reshape(rows, width),
        key_grad.astype(jnp.bfloat16).reshape(rows, width),
    )


def solution(mesh):
    return jax.shard_map(
        body,
        mesh=mesh,
        in_specs=(
            P("dp", "mp"), P(), P(None, "mp"), P("dp", "mp"), P("dp", "mp"), P("dp", "mp"), P(), P(),
        ),
        out_specs=(P("dp", "mp"), P("dp", "mp"), P("dp", "mp")),
        check_vma=False,
    )
```

```python
import jax
import jax.numpy as jnp
from jax import lax
from jax.experimental import pallas as pl
from jax.experimental.pallas import tpu as pltpu
from jax.sharding import PartitionSpec as P

HD = 128
MESH = pl.DeviceIdType.MESH
F32 = jnp.float32
BF16 = jnp.bfloat16
SIDE = 4
NZ = 8
NDP = 32
CHIPS = 16
ROWS = 512
CAP = 32
WIDTH = 384
PART = 192
TILE = 128
SPAN = 256
QUART = 48


def iota(shape, dim):
    return lax.broadcasted_iota(jnp.int32, shape, dim)


def dot(a, b, da, db):
    return lax.dot_general(a, b, (((da,), (db,)), ((), ())), preferred_element_type=F32)


def window(t):
    return jnp.clip(t * TILE - 64, 0, ROWS - SPAN)


def kernel(
    x_hbm, gain_ref, w_hbm, q_hbm, k_hbm, hc_hbm, owner_ref, count_ref,
    g_out, dq_out, dk_out,
    xg, w_v, q_v, k_v, cotr, cot_v, stat_src, stats, mean_v, rstd_v, idx_v, segc_v, segr_v,
    wts, vr_f, vr_b, vacc, n_v, pb, r0, s_v, dk_f, t_b,
    one_rel, one_raw, one_sum, one_out, two_rel, two_raw, two_sum, two_out,
    local_sem, ag_send, ag_recv, cot_send, cot_recv, st_send, st_recv, p_send, p_recv,
    rs_send, rs_recv,
):
    dp = lax.axis_index("dp")
    z = lax.axis_index("mp")
    core = lax.rem(dp, 2)
    chip = dp // 2
    px = chip // SIDE
    py = lax.rem(chip, SIDE)
    sibling = chip * 2 + 1 - core

    loads = [
        pltpu.make_async_copy(x_hbm.at[:, pl.ds(h * WIDTH, WIDTH)], xg.at[2 * z + h], local_sem.at[h])
        for h in range(2)
    ]
    loads += [
        pltpu.make_async_copy(q_hbm, q_v, local_sem.at[2]),
        pltpu.make_async_copy(k_hbm, k_v, local_sem.at[3]),
        pltpu.make_async_copy(w_hbm, w_v, local_sem.at[4]),
        pltpu.make_async_copy(
            hc_hbm.at[pl.ds(pl.multiple_of(dp * CAP, CAP), CAP)],
            cotr.at[pl.ds(pl.multiple_of(dp * CAP, CAP), CAP)], local_sem.at[5]),
    ]
    for load in loads:
        load.start()

    barrier = pltpu.get_barrier_semaphore()

    def greet_dp(j, carry):
        pl.semaphore_signal(barrier, inc=1, device_id={"dp": lax.rem(dp + j, NDP)}, device_id_type=MESH)
        return carry

    lax.fori_loop(1, NDP, greet_dp, 0)

    def greet_z(j, carry):
        pl.semaphore_signal(barrier, inc=1, device_id={"mp": lax.rem(z + j, NZ)}, device_id_type=MESH)
        return carry

    lax.fori_loop(1, NZ, greet_z, 0)
    pl.semaphore_wait(barrier, NDP - 1 + NZ - 1)

    def chunk_of(d, e):
        s = e // 2
        half = lax.rem(e + d, 2)
        origin = lax.rem(z + NZ + (2 * d - 1) * (s + 1), NZ)
        return origin * 2 + half

    def next_z(d):
        return lax.rem(z + NZ + 1 - 2 * d, NZ)

    def ag_copy(d, e, src):
        origin = lax.rem(z + NZ + (2 * d - 1) * (e // 2), NZ)
        ch = origin * 2 + lax.rem(e + d, 2)
        return pltpu.make_async_remote_copy(
            src_ref=xg.at[ch] if src is None else src, dst_ref=xg.at[ch],
            send_sem=ag_send.at[d, e], recv_sem=ag_recv.at[d, e],
            device_id={"mp": next_z(d)}, device_id_type=MESH)

    for d in range(2):
        ag_copy(d, 0, x_hbm.at[:, pl.ds(d * WIDTH, WIDTH)]).start()

    def cot_copy(j):
        to = lax.rem(dp + j, NDP)
        return pltpu.make_async_remote_copy(
            src_ref=hc_hbm.at[pl.ds(pl.multiple_of(to * CAP, CAP), CAP)],
            dst_ref=cotr.at[pl.ds(pl.multiple_of(dp * CAP, CAP), CAP)],
            send_sem=cot_send, recv_sem=cot_recv, device_id={"dp": to}, device_id_type=MESH)

    def start_cot(j, carry):
        cot_copy(j).start()
        return carry

    lax.fori_loop(1, NDP, start_cot, 0)

    loads[0].wait()
    loads[1].wait()
    width = 2 * WIDTH

    def stat_tile(i, carry):
        r = pl.ds(pl.multiple_of(i * TILE, TILE), TILE)
        xa = xg[2 * z, r, :].astype(F32)
        xb = xg[2 * z + 1, r, :].astype(F32)
        m = (jnp.sum(xa, axis=1, keepdims=True) + jnp.sum(xb, axis=1, keepdims=True)) / width
        xa = xa - m
        xb = xb - m
        m2 = jnp.sum(xa * xa, axis=1, keepdims=True) + jnp.sum(xb * xb, axis=1, keepdims=True)
        lane = iota((TILE, TILE), 1)
        both = jnp.where(lane == 0, m, jnp.where(lane == 1, m2, 0.0)).T
        stat_src[:, r] = both[0:8, :]
        return carry

    lax.fori_loop(0, ROWS // TILE, stat_tile, 0)

    row32 = iota((NDP, NDP), 0)
    col32 = iota((NDP, NDP), 1)
    mine = row32 == dp
    own_l = jnp.sum(jnp.where(mine, owner_ref[...].astype(F32), 0.0), axis=0, keepdims=True)
    cnt_l = jnp.sum(jnp.where(mine, count_ref[...].astype(F32), 0.0), axis=0, keepdims=True)
    cnt_s = jnp.sum(jnp.where(row32 == col32, cnt_l, 0.0), axis=1, keepdims=True)
    ends_l = jnp.sum(jnp.where(row32 <= col32, cnt_s, 0.0), axis=0, keepdims=True)
    ends_s = jnp.sum(jnp.where(col32 <= row32, cnt_l, 0.0), axis=1, keepdims=True)
    starts_l = ends_l - cnt_l
    row = iota((ROWS, NDP), 0).astype(F32)
    image = jnp.sum(jnp.where(ends_l <= row, 1.0, 0.0), axis=1, keepdims=True)
    picked = iota((ROWS, NDP), 1).astype(F32) == image
    row_owner = jnp.sum(jnp.where(picked, own_l, 0.0), axis=1, keepdims=True)
    row_start = jnp.sum(jnp.where(picked, starts_l, 0.0), axis=1, keepdims=True)
    idx_v[...] = row_owner * CAP + row[:, 0:1] - row_start
    segc_v[...] = image
    lane_row = iota((NDP, ROWS), 1).astype(F32)
    segr_v[...] = jnp.broadcast_to(
        jnp.sum(jnp.where(ends_s <= lane_row, 1.0, 0.0), axis=0, keepdims=True), (8, ROWS))

    def stat_copy(j):
        return pltpu.make_async_remote_copy(
            src_ref=stat_src, dst_ref=stats.at[z], send_sem=st_send, recv_sem=st_recv,
            device_id={"mp": lax.rem(z + j, NZ)}, device_id_type=MESH)

    def start_stat(j, carry):
        stat_copy(j).start()
        return carry

    lax.fori_loop(1, NZ, start_stat, 0)
    for d in range(2):
        ag_copy(d, 1, x_hbm.at[:, pl.ds((1 - d) * WIDTH, WIDTH)]).start()

    loads[2].wait()
    loads[3].wait()
    loads[5].wait()
    some = cotr.at[pl.ds(0, (NDP - 1) * CAP)]
    pltpu.make_async_copy(some, some, cot_recv).wait()

    def gather_tile(i, carry):
        r = pl.ds(pl.multiple_of(i * TILE, TILE), TILE)
        lane = iota((TILE, NDP * CAP), 1).astype(F32)
        onehot = jnp.where(lane == idx_v[r, :], 1.0, 0.0).astype(BF16)
        cot_v[r, :] = dot(onehot, cotr[...], 1, 0).astype(BF16)
        return carry

    lax.fori_loop(0, ROWS // TILE, gather_tile, 0)
    vr_f[...] = jnp.zeros_like(vr_f)
    vacc[...] = jnp.zeros_like(vacc)
    scale = HD ** (-0.5)
    tiles = ROWS // TILE
    heads = WIDTH // HD

    def forward(i, carry):
        h = i // tiles
        t = lax.rem(i, tiles)
        cols = pl.ds(pl.multiple_of(h * HD, HD), HD)
        r = pl.ds(pl.multiple_of(t * TILE, TILE), TILE)
        win = pl.ds(pl.multiple_of(window(t), 64), SPAN)
        st = dot(k_v[win, cols], q_v[r, cols], 1, 1) * scale
        st = jnp.where(segc_v[win, :] == segr_v[0:1, r], st, -1e9)
        e = jnp.exp(st - jnp.max(st, axis=0, keepdims=True))
        p = e / jnp.sum(e, axis=0, keepdims=True)
        wts[i] = p
        vr_f[win, cols] += dot(p.astype(BF16), cot_v[r, cols], 1, 0)
        return carry

    lax.fori_loop(0, heads * tiles, forward, 0)
    vr_b[...] = vr_f[...].astype(BF16)

    first = stats.at[pl.ds(0, NZ - 1)]
    pltpu.make_async_copy(first, first, st_recv).wait()
    stats[z] = stat_src[...]
    mean = sum(stats[i, 0:1, :] for i in range(NZ)) / NZ
    m2 = sum(stats[i, 1:2, :] + width * (stats[i, 0:1, :] - mean) ** 2 for i in range(NZ))
    rstd = lax.rsqrt(m2 / (width * NZ) + 1e-06)
    sub = iota((TILE, TILE), 0)
    for i in range(tiles):
        r = slice(i * TILE, (i + 1) * TILE)
        both = jnp.where(sub == 0, mean[:, r], jnp.where(sub == 1, rstd[:, r], 0.0)).T
        mean_v[r, :] = both[:, 0:1]
        rstd_v[r, :] = both[:, 1:2]
    loads[4].wait()

    def chunk_at(it):
        own = 2 * z + it
        a = jnp.maximum(it - 2, 0)
        return jnp.where(it < 2, own, chunk_of(lax.rem(a, 2), a // 2))

    def p_copy(it):
        ch = chunk_at(it)
        return pltpu.make_async_remote_copy(
            src_ref=pb.at[ch, pl.ds(pl.multiple_of((1 - core) * PART, 16), PART)], dst_ref=r0.at[ch],
            send_sem=p_send.at[it], recv_sem=p_recv.at[it],
            device_id={"dp": sibling}, device_id_type=MESH)

    def combine(it):
        p_copy(it).wait_recv()
        ch = chunk_at(it)
        mine = pb[ch, pl.ds(pl.multiple_of(core * PART, 16), PART), :].astype(F32)
        s_v[ch // SIDE, lax.rem(ch, SIDE)] = (mine + r0[ch].astype(F32)).astype(BF16)

    def arrive(it, carry):
        ch = chunk_at(it)

        @pl.when(it >= 2)
        def _():
            a = it - 2
            d = lax.rem(a, 2)
            e = a // 2
            pltpu.make_async_remote_copy(
                src_ref=xg.at[ch], dst_ref=xg.at[ch], send_sem=ag_send.at[d, e], recv_sem=ag_recv.at[d, e],
                device_id={"mp": next_z(d)}, device_id_type=MESH).wait_recv()

            @pl.when(e <= 4)
            def _():
                ag_copy(d, e + 2, None).start()

        @pl.when(it >= 1)
        def _():
            p_copy(it - 1).start()

        def norm_tile(i, c):
            r = pl.ds(pl.multiple_of(i * TILE, TILE), TILE)
            gain = gain_ref[:, pl.ds(pl.multiple_of(ch * WIDTH, HD), WIDTH)]
            xs = xg[ch, r, :].astype(F32)
            n_v[r, :] = ((xs - mean_v[r, :]) * rstd_v[r, :] * gain).astype(BF16)
            return c

        lax.fori_loop(0, ROWS // TILE, norm_tile, 0)
        vacc[...] += dot(n_v[...], w_v[pl.ds(pl.multiple_of(ch * WIDTH, HD), WIDTH), :], 1, 0)
        pb[ch] = dot(n_v[...], vr_b[...], 0, 0).astype(BF16)

        @pl.when(it >= 3)
        def _():
            combine(it - 3)

        return carry

    lax.fori_loop(0, CHIPS, arrive, 0)

    vr_b[...] = vacc[...].astype(BF16)
    p_copy(CHIPS - 1).start()
    dk_f[...] = jnp.zeros_like(dk_f)
    for it in range(CHIPS - 3, CHIPS):
        combine(it)

    def at_pos(axis, off):
        if axis == 0:
            return (lax.rem(px + SIDE + off, SIDE) * SIDE + py) * 2 + core
        return (px * SIDE + lax.rem(py + SIDE + off, SIDE)) * 2 + core

    def pos(axis, off):
        return lax.rem((px if axis == 0 else py) + SIDE + off, SIDE)

    class Ring:
        def __init__(self, half, phase):
            self.half, self.phase = half, phase
            self.axis = half if phase == 0 else 1 - half
            bufs = (one_rel, one_raw, one_sum, one_out) if phase == 0 else (two_rel, two_raw, two_sum, two_out)
            self.rel, self.raw, self.sum, self.out = [[b.at[half, d] for d in range(2)] for b in bufs]

        def src(self, off, quarter):
            if self.phase == 0:
                rows = pl.ds(self.half * 96 + quarter * QUART, QUART)
                where = pos(self.axis, off)
                return s_v.at[where, :, rows, :] if self.axis == 0 else s_v.at[:, where, rows, :]
            return t_b.at[self.half, pl.ds(pos(self.axis, off), 1), pl.ds(quarter * QUART, QUART), :]

        def copy(self, kind, d):
            step = 1 - 2 * d
            src, dst = {
                0: (lambda: self.src(2 * step, d), self.rel[d]),
                1: (lambda: self.src(step, 1 - d), self.raw[d]),
                2: (lambda: self.out[d], self.sum[d]),
            }[kind]
            k = ((self.half * 2 + self.phase) * 2 + d) * 3 + kind
            return pltpu.make_async_remote_copy(
                src_ref=src(), dst_ref=dst, send_sem=rs_send.at[k], recv_sem=rs_recv.at[k],
                device_id={"dp": at_pos(self.axis, step)}, device_id_type=MESH)

        def begin(self):
            for kind in (0, 1):
                for d in range(2):
                    self.copy(kind, d).start()

        def relay(self):
            for d in range(2):
                self.copy(0, d).wait_recv()
                step = 1 - 2 * d
                self.out[d][...] = (self.rel[d][...].astype(F32) + self.src(step, d)[...].astype(F32)).astype(BF16)
            for d in range(2):
                self.copy(2, d).start()

        def finish(self):
            res = []
            for d in range(2):
                self.copy(2, d).wait_recv()
                self.copy(1, 1 - d).wait_recv()
                res.append(
                    self.src(0, d)[...].astype(F32) + self.sum[d][...].astype(F32) + self.raw[1 - d][...].astype(F32))
            return res

        def drain(self):
            for kind in range(3):
                for d in range(2):
                    self.copy(kind, d).wait_send()

    def backward(h):
        cols = slice(h * HD, (h + 1) * HD)
        for t in range(tiles):
            r = slice(t * TILE, (t + 1) * TILE)
            lo = min(max(t * TILE - 64, 0), ROWS - SPAN)
            win = slice(lo, lo + SPAN)
            p = wts[h * tiles + t]
            dp_t = dot(vr_b[win, cols], cot_v[r, cols], 1, 1)
            centre = jnp.sum(p * dp_t, axis=0, keepdims=True)
            ds = (p * (dp_t - centre)).astype(BF16)
            dk_f[win, cols] += dot(ds, q_v[r, cols], 1, 0)
            dq_out[r, cols] = (dot(ds, k_v[win, cols], 0, 0) * scale).astype(BF16)

    one = [Ring(half, 0) for half in range(2)]
    two = [Ring(half, 1) for half in range(2)]
    for ring in one:
        ring.begin()
    backward(0)
    for ring in one:
        ring.relay()
    backward(1)
    for half in range(2):
        res = one[half].finish()
        for d in range(2):
            t_b[half, :, d * QUART:(d + 1) * QUART, :] = res[d].astype(BF16)
    backward(2)
    for ring in two:
        ring.begin()
    dk_out[...] = (dk_f[...] * scale).astype(BF16)
    for ring in two:
        ring.relay()
    for half in range(2):
        res = two[half].finish()
        for d in range(2):
            g_out[half * 96 + d * QUART:half * 96 + (d + 1) * QUART, :] = res[d][0]

    for ring in one + two:
        ring.drain()
    for d in range(2):
        for e in range(7):
            pltpu.make_async_remote_copy(
                src_ref=xg.at[0], dst_ref=xg.at[0], send_sem=ag_send.at[d, e], recv_sem=ag_recv.at[d, e],
                device_id={"mp": next_z(d)}, device_id_type=MESH).wait_send()
    for it in range(CHIPS):
        p_copy(it).wait_send()
    pltpu.make_async_copy(some, some, cot_send).wait()
    pltpu.make_async_copy(first, first, st_send).wait()


def body(
    patches, norm_gain, value_weight, queries, key_vectors, head_cotangent, image_owner, patch_count
):
    any_ = pl.BlockSpec(memory_space=pl.ANY)
    vmem = pl.BlockSpec(memory_space=pltpu.VMEM)
    V, DMA = pltpu.VMEM, pltpu.SemaphoreType.DMA
    one = V((2, 2, SIDE, QUART, WIDTH), BF16)
    two = V((2, 2, 1, QUART, WIDTH), BF16)
    return pl.pallas_call(
        kernel,
        out_shape=(
            jax.ShapeDtypeStruct((PART, WIDTH), F32),
            jax.ShapeDtypeStruct((ROWS, WIDTH), BF16),
            jax.ShapeDtypeStruct((ROWS, WIDTH), BF16),
        ),
        in_specs=[any_, vmem, any_, any_, any_, any_, vmem, vmem],
        out_specs=(vmem, vmem, vmem),
        scratch_shapes=[
            V((CHIPS, ROWS, WIDTH), BF16),
            V((NZ * 2 * WIDTH, WIDTH), BF16),
            V((ROWS, WIDTH), BF16),
            V((ROWS, WIDTH), BF16),
            V((NDP * CAP, WIDTH), BF16),
            V((ROWS, WIDTH), BF16),
            V((8, ROWS), F32),
            V((NZ, 8, ROWS), F32),
            V((ROWS, 1), F32),
            V((ROWS, 1), F32),
            V((ROWS, 1), F32),
            V((ROWS, 1), F32),
            V((8, ROWS), F32),
            V((3 * ROWS // TILE, SPAN, TILE), F32),
            V((ROWS, WIDTH), F32),
            V((ROWS, WIDTH), BF16),
            V((ROWS, WIDTH), F32),
            V((ROWS, WIDTH), BF16),
            V((CHIPS, 2 * PART, WIDTH), BF16),
            V((CHIPS, PART, WIDTH), BF16),
            V((SIDE, SIDE, PART, WIDTH), BF16),
            V((ROWS, WIDTH), F32),
            V((2, SIDE, 96, WIDTH), BF16),
            one, one, one, one, two, two, two, two,
            DMA((6,)), DMA((2, 7)), DMA((2, 7)), DMA, DMA, DMA, DMA, DMA((CHIPS,)), DMA((CHIPS,)),
            DMA((24,)), DMA((24,)),
        ],
        compiler_params=pltpu.CompilerParams(
            collective_id=0, has_side_effects=True, vmem_limit_bytes=60 * 1024 * 1024
        ),
    )(
        patches, norm_gain.reshape(1, -1), value_weight, queries, key_vectors, head_cotangent,
        image_owner, patch_count,
    )


def solution(mesh):
    return jax.shard_map(
        body,
        mesh=mesh,
        in_specs=(
            P("dp", "mp"), P(), P(None, "mp"), P("dp", "mp"), P("dp", "mp"), P("dp", "mp"), P(), P(),
        ),
        out_specs=(P("dp", "mp"), P("dp", "mp"), P("dp", "mp")),
        check_vma=False,
    )
```

```python
import jax
import jax.numpy as jnp
from jax import lax
from jax.experimental import pallas as pl
from jax.experimental.pallas import tpu as pltpu
from jax.sharding import PartitionSpec as P

HD = 128
MESH = pl.DeviceIdType.MESH
F32 = jnp.float32
BF16 = jnp.bfloat16
SIDE = 4
NZ = 8
NDP = 32
CHIPS = 16
ROWS = 512
CAP = 32
WIDTH = 384
PART = 192
TILE = 128
SPAN = 256
HALF = 96


def iota(shape, dim):
    return lax.broadcasted_iota(jnp.int32, shape, dim)


def dot(a, b, da, db):
    return lax.dot_general(a, b, (((da,), (db,)), ((), ())), preferred_element_type=F32)


def window(t):
    return jnp.clip(t * TILE - 64, 0, ROWS - SPAN)


def kernel(
    x_hbm, gain_hbm, w_hbm, q_hbm, k_hbm, hc_hbm, owner_hbm, count_hbm,
    g_hbm, dq_hbm, dk_hbm,
    gain_ref, owner_ref, count_ref, g_out, dq_out, dk_out,
    xg, w_v, q_v, k_v, cotr, cot_v, stat_src, stats, mean_v, rstd_v, idx_v, segc_v, segr_v,
    wts, vr_f, vr_b, vacc, n_v, pb, r0, s_v, dk_f, t_v, tree,
    local_sem, ag_send, ag_recv, cot_send, cot_recv, st_send, st_recv, p_send, p_recv,
    rs_send, rs_recv,
):
    dp = lax.axis_index("dp")
    z = lax.axis_index("mp")
    core = lax.rem(dp, 2)
    chip = dp // 2
    px = chip // SIDE
    py = lax.rem(chip, SIDE)
    sibling = chip * 2 + 1 - core

    loads = [
        pltpu.make_async_copy(x_hbm.at[:, pl.ds(h * WIDTH, WIDTH)], xg.at[2 * z + h], local_sem.at[h])
        for h in range(2)
    ]
    loads += [
        pltpu.make_async_copy(q_hbm, q_v, local_sem.at[2]),
        pltpu.make_async_copy(k_hbm, k_v, local_sem.at[3]),
        pltpu.make_async_copy(w_hbm, w_v, local_sem.at[4]),
        pltpu.make_async_copy(
            hc_hbm.at[pl.ds(pl.multiple_of(dp * CAP, CAP), CAP)],
            cotr.at[pl.ds(pl.multiple_of(dp * CAP, CAP), CAP)], local_sem.at[5]),
        pltpu.make_async_copy(owner_hbm, owner_ref, local_sem.at[6]),
        pltpu.make_async_copy(count_hbm, count_ref, local_sem.at[7]),
        pltpu.make_async_copy(gain_hbm, gain_ref, local_sem.at[8]),
    ]
    for load in loads:
        load.start()

    barrier = pltpu.get_barrier_semaphore()

    def greet_dp(j, carry):
        pl.semaphore_signal(barrier, inc=1, device_id={"dp": lax.rem(dp + j, NDP)}, device_id_type=MESH)
        return carry

    lax.fori_loop(1, NDP, greet_dp, 0)

    def greet_z(j, carry):
        pl.semaphore_signal(barrier, inc=1, device_id={"mp": lax.rem(z + j, NZ)}, device_id_type=MESH)
        return carry

    lax.fori_loop(1, NZ, greet_z, 0)
    pl.semaphore_wait(barrier, NDP - 1 + NZ - 1)

    def pair_chunk(j, d):
        origin = lax.rem(z + NZ + (2 * d - 1) * ((j + 1) // 2), NZ)
        return origin * 2 + lax.rem(j + 1 + d, 2)

    def next_z(d):
        return lax.rem(z + NZ + 1 - 2 * d, NZ)

    def ag_copy(d, e, src):
        origin = lax.rem(z + NZ + (2 * d - 1) * (e // 2), NZ)
        ch = origin * 2 + lax.rem(e + d, 2)
        return pltpu.make_async_remote_copy(
            src_ref=xg.at[ch] if src is None else src, dst_ref=xg.at[ch],
            send_sem=ag_send.at[d, e], recv_sem=ag_recv.at[d, e],
            device_id={"mp": next_z(d)}, device_id_type=MESH)

    for d in range(2):
        ag_copy(d, 0, x_hbm.at[:, pl.ds(d * WIDTH, WIDTH)]).start()

    def cot_copy(j):
        to = lax.rem(dp + j, NDP)
        return pltpu.make_async_remote_copy(
            src_ref=hc_hbm.at[pl.ds(pl.multiple_of(to * CAP, CAP), CAP)],
            dst_ref=cotr.at[pl.ds(pl.multiple_of(dp * CAP, CAP), CAP)],
            send_sem=cot_send, recv_sem=cot_recv, device_id={"dp": to}, device_id_type=MESH)

    def start_cot(j, carry):
        cot_copy(j).start()
        return carry

    lax.fori_loop(1, NDP, start_cot, 0)

    loads[0].wait()
    loads[1].wait()
    width = 2 * WIDTH
    tiles = ROWS // TILE

    def stat_tile(i, carry):
        r = pl.ds(pl.multiple_of(i * TILE, TILE), TILE)
        xa = xg[2 * z, r, :].astype(F32)
        xb = xg[2 * z + 1, r, :].astype(F32)
        m = (jnp.sum(xa, axis=1, keepdims=True) + jnp.sum(xb, axis=1, keepdims=True)) / width
        xa = xa - m
        xb = xb - m
        m2 = jnp.sum(xa * xa, axis=1, keepdims=True) + jnp.sum(xb * xb, axis=1, keepdims=True)
        lane = iota((TILE, TILE), 1)
        both = jnp.where(lane == 0, m, jnp.where(lane == 1, m2, 0.0)).T
        stat_src[pl.ds(i, 1), :] = both[0:1, :]
        stat_src[pl.ds(tiles + i, 1), :] = both[1:2, :]
        return carry

    lax.fori_loop(0, ROWS // TILE, stat_tile, 0)

    loads[6].wait()
    loads[7].wait()

    row32 = iota((NDP, NDP), 0)
    col32 = iota((NDP, NDP), 1)
    mine = row32 == dp
    own_l = jnp.sum(jnp.where(mine, owner_ref[...].astype(F32), 0.0), axis=0, keepdims=True)
    cnt_l = jnp.sum(jnp.where(mine, count_ref[...].astype(F32), 0.0), axis=0, keepdims=True)
    cnt_s = jnp.sum(jnp.where(row32 == col32, cnt_l, 0.0), axis=1, keepdims=True)
    ends_l = jnp.sum(jnp.where(row32 <= col32, cnt_s, 0.0), axis=0, keepdims=True)
    ends_s = jnp.sum(jnp.where(col32 <= row32, cnt_l, 0.0), axis=1, keepdims=True)
    starts_l = ends_l - cnt_l
    row = iota((ROWS, NDP), 0).astype(F32)
    image = jnp.sum(jnp.where(ends_l <= row, 1.0, 0.0), axis=1, keepdims=True)
    picked = iota((ROWS, NDP), 1).astype(F32) == image
    row_owner = jnp.sum(jnp.where(picked, own_l, 0.0), axis=1, keepdims=True)
    row_start = jnp.sum(jnp.where(picked, starts_l, 0.0), axis=1, keepdims=True)
    idx_v[...] = row_owner * CAP + row[:, 0:1] - row_start
    segc_v[...] = image
    lane_row = iota((NDP, ROWS), 1).astype(F32)
    segr_v[...] = jnp.broadcast_to(
        jnp.sum(jnp.where(ends_s <= lane_row, 1.0, 0.0), axis=0, keepdims=True), (8, ROWS))

    def stat_copy(j):
        return pltpu.make_async_remote_copy(
            src_ref=stat_src, dst_ref=stats.at[z], send_sem=st_send, recv_sem=st_recv,
            device_id={"mp": lax.rem(z + j, NZ)}, device_id_type=MESH)

    def start_stat(j, carry):
        stat_copy(j).start()
        return carry

    lax.fori_loop(1, NZ, start_stat, 0)
    for d in range(2):
        ag_copy(d, 1, x_hbm.at[:, pl.ds((1 - d) * WIDTH, WIDTH)]).start()

    def arrival(j):
        for d in range(2):
            ch = pair_chunk(j, d)
            pltpu.make_async_remote_copy(
                src_ref=xg.at[ch], dst_ref=xg.at[ch], send_sem=ag_send.at[d, j - 1],
                recv_sem=ag_recv.at[d, j - 1], device_id={"mp": next_z(d)}, device_id_type=MESH).wait_recv()

            @pl.when(j <= NZ - 3)
            def _():
                ag_copy(d, j + 1, None).start()

    arrival(1)

    loads[2].wait()
    loads[3].wait()
    loads[5].wait()
    some = cotr.at[pl.ds(0, (NDP - 1) * CAP)]
    pltpu.make_async_copy(some, some, cot_recv).wait()

    def gather_tile(i, carry):
        r = pl.ds(pl.multiple_of(i * TILE, TILE), TILE)
        lane = iota((TILE, NDP * CAP), 1).astype(F32)
        onehot = jnp.where(lane == idx_v[r, :], 1.0, 0.0).astype(BF16)
        cot_v[r, :] = dot(onehot, cotr[...], 1, 0).astype(BF16)
        return carry

    lax.fori_loop(0, ROWS // TILE, gather_tile, 0)
    vr_f[...] = jnp.zeros_like(vr_f)
    vacc[...] = jnp.zeros_like(vacc)
    scale = HD ** (-0.5)
    heads = WIDTH // HD

    def forward(i, carry):
        h = i // tiles
        t = lax.rem(i, tiles)
        cols = pl.ds(pl.multiple_of(h * HD, HD), HD)
        r = pl.ds(pl.multiple_of(t * TILE, TILE), TILE)
        win = pl.ds(pl.multiple_of(window(t), 64), SPAN)
        st = dot(k_v[win, cols], q_v[r, cols], 1, 1) * scale
        st = jnp.where(segc_v[win, :] == segr_v[0:1, r], st, -1e9)
        e = jnp.exp(st - jnp.max(st, axis=0, keepdims=True))
        p = e / jnp.sum(e, axis=0, keepdims=True)
        wts[i] = p
        vr_f[win, cols] += dot(p.astype(BF16), cot_v[r, cols], 1, 0)
        return carry

    lax.fori_loop(0, heads * tiles, forward, 0)
    vr_b[...] = vr_f[...].astype(BF16)
    arrival(2)

    first = stats.at[pl.ds(0, NZ - 1)]
    pltpu.make_async_copy(first, first, st_recv).wait()
    stats[z] = stat_src[...]
    mean = sum(stats[i, 0:tiles, :] for i in range(NZ)) / NZ
    m2 = sum(stats[i, tiles:8, :] + width * (stats[i, 0:tiles, :] - mean) ** 2 for i in range(NZ))
    rstd = lax.rsqrt(m2 / (width * NZ) + 1e-06)
    sub = iota((TILE, TILE), 0)
    for i in range(tiles):
        r = slice(i * TILE, (i + 1) * TILE)
        both = jnp.where(sub == 0, mean[i:i + 1, :], jnp.where(sub == 1, rstd[i:i + 1, :], 0.0)).T
        mean_v[r, :] = both[:, 0:1]
        rstd_v[r, :] = both[:, 1:2]
    loads[4].wait()
    loads[8].wait()

    def p_copy(j, d):
        ch = pair_chunk(j, d)
        return pltpu.make_async_remote_copy(
            src_ref=pb.at[ch, pl.ds(pl.multiple_of((1 - core) * PART, 16), PART)], dst_ref=r0.at[ch],
            send_sem=p_send.at[j, d], recv_sem=p_recv.at[j, d],
            device_id={"dp": sibling}, device_id_type=MESH)

    def at_pos(axis, off):
        if axis == 0:
            return (lax.rem(px + SIDE + off, SIDE) * SIDE + py) * 2 + core
        return (px * SIDE + lax.rem(py + SIDE + off, SIDE)) * 2 + core

    class Tree:
        def __init__(self, j, d, stage):
            self.j, self.d, self.stage = j, d, stage
            ch = pair_chunk(j, d)
            self.axis = 1 - d if stage == 0 else d
            place, goal = (px, py), (ch // SIDE, lax.rem(ch, SIDE))
            self.r = lax.rem(place[self.axis] + SIDE - goal[self.axis], SIDE)
            self.here = place[1 - self.axis] == goal[1 - self.axis] if stage else px >= 0
            self.src = s_v.at[ch] if stage == 0 else t_v.at[j, d]
            self.slots = tree.at[j, d, stage]
            self.low = self.r // 2
            self.sgn = 2 * self.low - 1

        def half(self, h):
            return pl.ds(pl.multiple_of(h * HALF, 16), HALF)

        def copy(self, src, off, slot, i):
            return pltpu.make_async_remote_copy(
                src_ref=src, dst_ref=self.slots.at[slot],
                send_sem=rs_send.at[self.j, self.d, self.stage, i],
                recv_sem=rs_recv.at[self.j, self.d, self.stage, slot],
                device_id={"dp": at_pos(self.axis, off)}, device_id_type=MESH)

        def is_far(self):
            return jnp.logical_and(self.here, self.r == 2)

        def is_near(self):
            return jnp.logical_and(self.here, lax.rem(self.r, 2) == 1)

        def is_goal(self):
            return jnp.logical_and(self.here, self.r == 0)

        def far(self):
            return [self.copy(self.src.at[self.half(0)], -1, 0, 0), self.copy(self.src.at[self.half(1)], 1, 0, 1)]

        def raw(self):
            return self.copy(self.src.at[self.half(1 - self.low)], self.sgn, 1 + self.low, 0)

        def total(self):
            return self.copy(self.slots.at[1], self.sgn, 3 * self.low, 1)

        def begin(self):
            @pl.when(self.is_far())
            def _():
                for c in self.far():
                    c.start()

            @pl.when(self.is_near())
            def _():
                self.raw().start()

        def relay(self):
            @pl.when(self.is_near())
            def _():
                self.copy(self.slots.at[0], 1, 0, 0).wait_recv()
                self.slots[1] = (self.slots[0].astype(F32) + self.src[self.half(self.low), :].astype(F32)).astype(BF16)
                self.total().start()

        def finish(self):
            @pl.when(self.is_goal())
            def _():
                for i in range(4):
                    self.copy(self.slots.at[i], 1, i, 0).wait_recv()
                for h in range(2):
                    rows = slice(h * HALF, (h + 1) * HALF)
                    res = (
                        self.src[rows, :].astype(F32) + self.slots[h].astype(F32) + self.slots[2 + h].astype(F32))
                    if self.stage == 0:
                        t_v[self.j, self.d, rows, :] = res.astype(BF16)
                    else:
                        g_out[rows, :] = res

        def drain(self):
            @pl.when(self.is_far())
            def _():
                for c in self.far():
                    c.wait_send()

            @pl.when(self.is_near())
            def _():
                self.raw().wait_send()
                self.total().wait_send()

    def trees(j, stage):
        return [Tree(j, d, stage) for d in range(2)]

    def combine(j):
        for d in range(2):
            p_copy(j, d).wait_recv()
            ch = pair_chunk(j, d)
            mine = pb[ch, pl.ds(pl.multiple_of(core * PART, 16), PART), :].astype(F32)
            s_v[ch] = (mine + r0[ch].astype(F32)).astype(BF16)
        for t in trees(j, 0):
            t.begin()

    def second(j):
        for t in trees(j, 0):
            t.finish()
        for t in trees(j, 1):
            t.begin()

    def relay(j, stage):
        for t in trees(j, stage):
            t.relay()

    def last(j):
        for t in trees(j, 1):
            t.finish()

    def pair(j, carry):
        @pl.when(j >= 3)
        def _():
            arrival(j)

        for d in range(2):
            ch = pair_chunk(j, d)

            def norm_tile(i, c):
                r = pl.ds(pl.multiple_of(i * TILE, TILE), TILE)
                gain = gain_ref[:, pl.ds(pl.multiple_of(ch * WIDTH, HD), WIDTH)]
                xs = xg[ch, r, :].astype(F32)
                n_v[d, r, :] = ((xs - mean_v[r, :]) * rstd_v[r, :] * gain).astype(BF16)
                return c

            lax.fori_loop(0, ROWS // TILE, norm_tile, 0)
            pb[ch] = dot(n_v[d], vr_b[...], 0, 0).astype(BF16)
        for d in range(2):
            p_copy(j, d).start()
            ch = pair_chunk(j, d)
            vacc[...] += dot(n_v[d], w_v[pl.ds(pl.multiple_of(ch * WIDTH, HD), WIDTH), :], 1, 0)

        @pl.when(j >= 1)
        def _():
            combine(j - 1)

        @pl.when(j >= 2)
        def _():
            relay(j - 2, 0)

        @pl.when(j >= 3)
        def _():
            second(j - 3)

        @pl.when(j >= 4)
        def _():
            relay(j - 4, 1)

        @pl.when(j >= 5)
        def _():
            last(j - 5)

        return carry

    lax.fori_loop(0, NZ, pair, 0)

    def backward(h):
        cols = slice(h * HD, (h + 1) * HD)
        for t in range(tiles):
            r = slice(t * TILE, (t + 1) * TILE)
            lo = min(max(t * TILE - 64, 0), ROWS - SPAN)
            win = slice(lo, lo + SPAN)
            p = wts[h * tiles + t]
            dp_t = dot(vr_b[win, cols], cot_v[r, cols], 1, 1)
            centre = jnp.sum(p * dp_t, axis=0, keepdims=True)
            ds = (p * (dp_t - centre)).astype(BF16)
            dk_f[win, cols] += dot(ds, q_v[r, cols], 1, 0)
            dq_out[r, cols] = (dot(ds, k_v[win, cols], 0, 0) * scale).astype(BF16)

    vr_b[...] = vacc[...].astype(BF16)
    dk_f[...] = jnp.zeros_like(dk_f)
    combine(NZ - 1)
    relay(NZ - 2, 0)
    second(NZ - 3)
    relay(NZ - 4, 1)
    last(NZ - 5)
    backward(0)
    relay(NZ - 1, 0)
    second(NZ - 2)
    relay(NZ - 3, 1)
    last(NZ - 4)
    backward(1)
    second(NZ - 1)
    relay(NZ - 2, 1)
    last(NZ - 3)
    backward(2)
    dk_out[...] = (dk_f[...] * scale).astype(BF16)
    stores = [
        pltpu.make_async_copy(dq_out, dq_hbm, local_sem.at[0]),
        pltpu.make_async_copy(dk_out, dk_hbm, local_sem.at[1]),
        pltpu.make_async_copy(g_out, g_hbm, local_sem.at[2]),
    ]
    stores[0].start()
    stores[1].start()
    relay(NZ - 1, 1)
    last(NZ - 2)
    last(NZ - 1)
    stores[2].start()

    def drain(j, carry):
        for stage in range(2):
            for t in trees(j, stage):
                t.drain()
        for d in range(2):
            p_copy(j, d).wait_send()
        return carry

    lax.fori_loop(0, NZ, drain, 0)
    for d in range(2):
        for e in range(7):
            pltpu.make_async_remote_copy(
                src_ref=xg.at[0], dst_ref=xg.at[0], send_sem=ag_send.at[d, e], recv_sem=ag_recv.at[d, e],
                device_id={"mp": next_z(d)}, device_id_type=MESH).wait_send()
    pltpu.make_async_copy(some, some, cot_send).wait()
    pltpu.make_async_copy(first, first, st_send).wait()
    for store in stores:
        store.wait()


def body(
    patches, norm_gain, value_weight, queries, key_vectors, head_cotangent, image_owner, patch_count
):
    any_ = pl.BlockSpec(memory_space=pl.ANY)
    V, DMA = pltpu.VMEM, pltpu.SemaphoreType.DMA
    return pl.pallas_call(
        kernel,
        out_shape=(
            jax.ShapeDtypeStruct((PART, WIDTH), F32),
            jax.ShapeDtypeStruct((ROWS, WIDTH), BF16),
            jax.ShapeDtypeStruct((ROWS, WIDTH), BF16),
        ),
        in_specs=[any_] * 8,
        out_specs=(any_,) * 3,
        scratch_shapes=[
            V((1, NZ * 2 * WIDTH), F32),
            V((NDP, NDP), jnp.int32),
            V((NDP, NDP), jnp.int32),
            V((PART, WIDTH), F32),
            V((ROWS, WIDTH), BF16),
            V((ROWS, WIDTH), BF16),
            V((CHIPS, ROWS, WIDTH), BF16),
            V((NZ * 2 * WIDTH, WIDTH), BF16),
            V((ROWS, WIDTH), BF16),
            V((ROWS, WIDTH), BF16),
            V((NDP * CAP, WIDTH), BF16),
            V((ROWS, WIDTH), BF16),
            V((8, TILE), F32),
            V((NZ, 8, TILE), F32),
            V((ROWS, 1), F32),
            V((ROWS, 1), F32),
            V((ROWS, 1), F32),
            V((ROWS, 1), F32),
            V((8, ROWS), F32),
            V((3 * ROWS // TILE, SPAN, TILE), F32),
            V((ROWS, WIDTH), F32),
            V((ROWS, WIDTH), BF16),
            V((ROWS, WIDTH), F32),
            V((2, ROWS, WIDTH), BF16),
            V((CHIPS, 2 * PART, WIDTH), BF16),
            V((CHIPS, PART, WIDTH), BF16),
            V((CHIPS, PART, WIDTH), BF16),
            V((ROWS, WIDTH), F32),
            V((NZ, 2, PART, WIDTH), BF16),
            V((NZ, 2, 2, 4, HALF, WIDTH), BF16),
            DMA((9,)), DMA((2, 7)), DMA((2, 7)), DMA, DMA, DMA, DMA, DMA((NZ, 2)), DMA((NZ, 2)),
            DMA((NZ, 2, 2, 2)), DMA((NZ, 2, 2, 4)),
        ],
        compiler_params=pltpu.CompilerParams(
            collective_id=0, has_side_effects=True, vmem_limit_bytes=60 * 1024 * 1024
        ),
    )(
        patches, norm_gain.reshape(1, -1), value_weight, queries, key_vectors, head_cotangent,
        image_owner, patch_count,
    )


def solution(mesh):
    return jax.shard_map(
        body,
        mesh=mesh,
        in_specs=(
            P("dp", "mp"), P(), P(None, "mp"), P("dp", "mp"), P("dp", "mp"), P("dp", "mp"), P(), P(),
        ),
        out_specs=(P("dp", "mp"), P("dp", "mp"), P("dp", "mp")),
        check_vma=False,
    )
```

```python
import jax
import jax.numpy as jnp
from jax import lax
from jax.experimental import pallas as pl
from jax.experimental.pallas import tpu as pltpu
from jax.sharding import PartitionSpec as P

HD = 128
MESH = pl.DeviceIdType.MESH
F32 = jnp.float32
BF16 = jnp.bfloat16
SIDE = 4
NZ = 8
NDP = 32
CHIPS = 16
ROWS = 512
CAP = 32
WIDTH = 384
PART = 192
TILE = 128
SPAN = 256
LAST_PARTS = 3


def iota(shape, dim):
    return lax.broadcasted_iota(jnp.int32, shape, dim)


def dot(a, b, da, db):
    return lax.dot_general(a, b, (((da,), (db,)), ((), ())), preferred_element_type=F32)


def window(t):
    return jnp.clip(t * TILE - 64, 0, ROWS - SPAN)


def kernel(
    x_hbm, gain_hbm, w_hbm, q_hbm, k_hbm, hc_hbm, owner_hbm, count_hbm,
    g_hbm, dq_hbm, dk_hbm,
    gain_ref, owner_ref, count_ref, g_out, dq_out, dk_out,
    xg, w_v, q_v, k_v, cotr, cot_v, stat_src, stats, mean_v, rstd_v, idx_v, segc_v, segr_v,
    wts, vr_f, vr_b, vacc, n_v, pb, r0, s_v, dk_f, t_v, tree,
    local_sem, ag_send, ag_recv, cot_send, cot_recv, st_send, st_recv, p_send, p_recv,
    rs_send, rs_recv, end_tree, end_send, end_recv,
):
    dp = lax.axis_index("dp")
    z = lax.axis_index("mp")
    core = lax.rem(dp, 2)
    chip = dp // 2
    px = chip // SIDE
    py = lax.rem(chip, SIDE)
    sibling = chip * 2 + 1 - core

    loads = [
        pltpu.make_async_copy(x_hbm.at[:, pl.ds(h * WIDTH, WIDTH)], xg.at[2 * z + h], local_sem.at[h])
        for h in range(2)
    ]
    loads += [
        pltpu.make_async_copy(q_hbm, q_v, local_sem.at[2]),
        pltpu.make_async_copy(k_hbm, k_v, local_sem.at[3]),
        pltpu.make_async_copy(w_hbm, w_v, local_sem.at[4]),
        pltpu.make_async_copy(
            hc_hbm.at[pl.ds(pl.multiple_of(dp * CAP, CAP), CAP)],
            cotr.at[pl.ds(pl.multiple_of(dp * CAP, CAP), CAP)], local_sem.at[5]),
        pltpu.make_async_copy(owner_hbm, owner_ref, local_sem.at[6]),
        pltpu.make_async_copy(count_hbm, count_ref, local_sem.at[7]),
        pltpu.make_async_copy(gain_hbm, gain_ref, local_sem.at[8]),
    ]
    for load in loads:
        load.start()

    barrier = pltpu.get_barrier_semaphore()

    def greet_dp(j, carry):
        pl.semaphore_signal(barrier, inc=1, device_id={"dp": lax.rem(dp + j, NDP)}, device_id_type=MESH)
        return carry

    lax.fori_loop(1, NDP, greet_dp, 0)

    def greet_z(j, carry):
        pl.semaphore_signal(barrier, inc=1, device_id={"mp": lax.rem(z + j, NZ)}, device_id_type=MESH)
        return carry

    lax.fori_loop(1, NZ, greet_z, 0)
    pl.semaphore_wait(barrier, NDP - 1 + NZ - 1)

    def pair_chunk(j, d):
        origin = lax.rem(z + NZ + (2 * d - 1) * ((j + 1) // 2), NZ)
        return origin * 2 + lax.rem(j + 1 + d, 2)

    def next_z(d):
        return lax.rem(z + NZ + 1 - 2 * d, NZ)

    def ag_copy(d, e, src):
        origin = lax.rem(z + NZ + (2 * d - 1) * (e // 2), NZ)
        ch = origin * 2 + lax.rem(e + d, 2)
        return pltpu.make_async_remote_copy(
            src_ref=xg.at[ch] if src is None else src, dst_ref=xg.at[ch],
            send_sem=ag_send, recv_sem=ag_recv.at[d, e],
            device_id={"mp": next_z(d)}, device_id_type=MESH)

    for d in range(2):
        ag_copy(d, 0, x_hbm.at[:, pl.ds(d * WIDTH, WIDTH)]).start()

    def cot_copy(j):
        to = lax.rem(dp + j, NDP)
        return pltpu.make_async_remote_copy(
            src_ref=hc_hbm.at[pl.ds(pl.multiple_of(to * CAP, CAP), CAP)],
            dst_ref=cotr.at[pl.ds(pl.multiple_of(dp * CAP, CAP), CAP)],
            send_sem=cot_send, recv_sem=cot_recv, device_id={"dp": to}, device_id_type=MESH)

    def start_cot(j, carry):
        cot_copy(j).start()
        return carry

    lax.fori_loop(1, NDP, start_cot, 0)

    loads[0].wait()
    loads[1].wait()
    width = 2 * WIDTH
    tiles = ROWS // TILE

    def stat_tile(i, carry):
        r = pl.ds(pl.multiple_of(i * TILE, TILE), TILE)
        xa = xg[2 * z, r, :].astype(F32)
        xb = xg[2 * z + 1, r, :].astype(F32)
        m = (jnp.sum(xa, axis=1, keepdims=True) + jnp.sum(xb, axis=1, keepdims=True)) / width
        xa = xa - m
        xb = xb - m
        m2 = jnp.sum(xa * xa, axis=1, keepdims=True) + jnp.sum(xb * xb, axis=1, keepdims=True)
        lane = iota((TILE, TILE), 1)
        both = jnp.where(lane == 0, m, jnp.where(lane == 1, m2, 0.0)).T
        stat_src[pl.ds(i, 1), :] = both[0:1, :]
        stat_src[pl.ds(tiles + i, 1), :] = both[1:2, :]
        return carry

    lax.fori_loop(0, ROWS // TILE, stat_tile, 0)

    loads[6].wait()
    loads[7].wait()

    row32 = iota((NDP, NDP), 0)
    col32 = iota((NDP, NDP), 1)
    mine = row32 == dp
    own_l = jnp.sum(jnp.where(mine, owner_ref[...].astype(F32), 0.0), axis=0, keepdims=True)
    cnt_l = jnp.sum(jnp.where(mine, count_ref[...].astype(F32), 0.0), axis=0, keepdims=True)
    cnt_s = jnp.sum(jnp.where(row32 == col32, cnt_l, 0.0), axis=1, keepdims=True)
    ends_l = jnp.sum(jnp.where(row32 <= col32, cnt_s, 0.0), axis=0, keepdims=True)
    ends_s = jnp.sum(jnp.where(col32 <= row32, cnt_l, 0.0), axis=1, keepdims=True)
    starts_l = ends_l - cnt_l
    row = iota((ROWS, NDP), 0).astype(F32)
    image = jnp.sum(jnp.where(ends_l <= row, 1.0, 0.0), axis=1, keepdims=True)
    picked = iota((ROWS, NDP), 1).astype(F32) == image
    row_owner = jnp.sum(jnp.where(picked, own_l, 0.0), axis=1, keepdims=True)
    row_start = jnp.sum(jnp.where(picked, starts_l, 0.0), axis=1, keepdims=True)
    idx_v[...] = row_owner * CAP + row[:, 0:1] - row_start
    segc_v[...] = image
    lane_row = iota((NDP, ROWS), 1).astype(F32)
    segr_v[...] = jnp.broadcast_to(
        jnp.sum(jnp.where(ends_s <= lane_row, 1.0, 0.0), axis=0, keepdims=True), (8, ROWS))

    def stat_copy(j):
        return pltpu.make_async_remote_copy(
            src_ref=stat_src, dst_ref=stats.at[z], send_sem=st_send, recv_sem=st_recv,
            device_id={"mp": lax.rem(z + j, NZ)}, device_id_type=MESH)

    def start_stat(j, carry):
        stat_copy(j).start()
        return carry

    lax.fori_loop(1, NZ, start_stat, 0)
    for d in range(2):
        ag_copy(d, 1, x_hbm.at[:, pl.ds((1 - d) * WIDTH, WIDTH)]).start()

    def arrival(j):
        for d in range(2):
            ch = pair_chunk(j, d)
            pltpu.make_async_remote_copy(
                src_ref=xg.at[ch], dst_ref=xg.at[ch], send_sem=ag_send,
                recv_sem=ag_recv.at[d, j - 1], device_id={"mp": next_z(d)}, device_id_type=MESH).wait_recv()

            @pl.when(j <= NZ - 3)
            def _():
                ag_copy(d, j + 1, None).start()

    arrival(1)

    loads[2].wait()
    loads[3].wait()
    loads[5].wait()
    some = cotr.at[pl.ds(0, (NDP - 1) * CAP)]
    pltpu.make_async_copy(some, some, cot_recv).wait()

    def gather_tile(i, carry):
        r = pl.ds(pl.multiple_of(i * TILE, TILE), TILE)
        lane = iota((TILE, NDP * CAP), 1).astype(F32)
        onehot = jnp.where(lane == idx_v[r, :], 1.0, 0.0).astype(BF16)
        cot_v[r, :] = dot(onehot, cotr[...], 1, 0).astype(BF16)
        return carry

    lax.fori_loop(0, ROWS // TILE, gather_tile, 0)
    vr_f[...] = jnp.zeros_like(vr_f)
    vacc[...] = jnp.zeros_like(vacc)
    scale = HD ** (-0.5)
    heads = WIDTH // HD

    def forward(i, carry):
        h = i // tiles
        t = lax.rem(i, tiles)
        cols = pl.ds(pl.multiple_of(h * HD, HD), HD)
        r = pl.ds(pl.multiple_of(t * TILE, TILE), TILE)
        win = pl.ds(pl.multiple_of(window(t), 64), SPAN)
        st = dot(k_v[win, cols], q_v[r, cols], 1, 1) * scale
        st = jnp.where(segc_v[win, :] == segr_v[0:1, r], st, -1e9)
        e = jnp.exp(st - jnp.max(st, axis=0, keepdims=True))
        p = e / jnp.sum(e, axis=0, keepdims=True)
        wts[i] = p
        vr_f[win, cols] += dot(p.astype(BF16), cot_v[r, cols], 1, 0)
        return carry

    lax.fori_loop(0, heads * tiles, forward, 0)
    vr_b[...] = vr_f[...].astype(BF16)
    arrival(2)

    first = stats.at[pl.ds(0, NZ - 1)]
    pltpu.make_async_copy(first, first, st_recv).wait()
    stats[z] = stat_src[...]
    mean = sum(stats[i, 0:tiles, :] for i in range(NZ)) / NZ
    m2 = sum(stats[i, tiles:8, :] + width * (stats[i, 0:tiles, :] - mean) ** 2 for i in range(NZ))
    rstd = lax.rsqrt(m2 / (width * NZ) + 1e-06)
    sub = iota((TILE, TILE), 0)
    for i in range(tiles):
        r = slice(i * TILE, (i + 1) * TILE)
        both = jnp.where(sub == 0, mean[i:i + 1, :], jnp.where(sub == 1, rstd[i:i + 1, :], 0.0)).T
        mean_v[r, :] = both[:, 0:1]
        rstd_v[r, :] = both[:, 1:2]
    loads[4].wait()
    loads[8].wait()

    def p_copy(j, d):
        ch = pair_chunk(j, d)
        return pltpu.make_async_remote_copy(
            src_ref=pb.at[ch, pl.ds(pl.multiple_of((1 - core) * PART, 16), PART)], dst_ref=r0.at[ch],
            send_sem=p_send, recv_sem=p_recv.at[j],
            device_id={"dp": sibling}, device_id_type=MESH)

    def at_pos(axis, off):
        if axis == 0:
            return (lax.rem(px + SIDE + off, SIDE) * SIDE + py) * 2 + core
        return (px * SIDE + lax.rem(py + SIDE + off, SIDE)) * 2 + core

    class Tree:
        def __init__(self, j, d, part, stage):
            self.j, self.d, self.stage = j, d, stage
            if part is None:
                self.base, self.size = 0, PART // 2
                self.slots, self.send, self.recv = tree.at[j, d, stage], rs_send.at[j, d, stage], rs_recv.at[j, d, stage]
            else:
                self.size = PART // LAST_PARTS // 2
                self.base = part * 2 * self.size
                self.slots = end_tree.at[d, part, stage]
                self.send, self.recv = end_send.at[d, part, stage], end_recv.at[d, part, stage]
            ch = pair_chunk(j, d)
            self.axis = 1 - d if stage == 0 else d
            place, goal = (px, py), (ch // SIDE, lax.rem(ch, SIDE))
            self.r = lax.rem(place[self.axis] + SIDE - goal[self.axis], SIDE)
            self.here = place[1 - self.axis] == goal[1 - self.axis] if stage else px >= 0
            self.src = s_v.at[ch] if stage == 0 else t_v.at[j, d]
            self.low = self.r // 2
            self.sgn = 2 * self.low - 1

        def half(self, h):
            return pl.ds(pl.multiple_of(self.base + h * self.size, 16), self.size)

        def copy(self, src, off, slot):
            return pltpu.make_async_remote_copy(
                src_ref=src, dst_ref=self.slots.at[slot], send_sem=self.send, recv_sem=self.recv,
                device_id={"dp": at_pos(self.axis, off)}, device_id_type=MESH)

        def is_far(self):
            return jnp.logical_and(self.here, self.r == 2)

        def is_near(self):
            return jnp.logical_and(self.here, lax.rem(self.r, 2) == 1)

        def is_goal(self):
            return jnp.logical_and(self.here, self.r == 0)

        def far(self):
            return [self.copy(self.src.at[self.half(0)], -1, 0), self.copy(self.src.at[self.half(1)], 1, 0)]

        def raw(self):
            return self.copy(self.src.at[self.half(1 - self.low)], self.sgn, 1 + self.low)

        def total(self):
            return self.copy(self.slots.at[1], self.sgn, 3 * self.low)

        def begin(self):
            @pl.when(self.is_far())
            def _():
                for c in self.far():
                    c.start()

            @pl.when(self.is_near())
            def _():
                self.raw().start()

        def relay(self):
            @pl.when(self.is_near())
            def _():
                self.copy(self.slots.at[0], 1, 0).wait_recv()
                self.slots[1] = (self.slots[0].astype(F32) + self.src[self.half(self.low), :].astype(F32)).astype(BF16)
                self.total().start()

        def finish(self):
            @pl.when(self.is_goal())
            def _():
                pltpu.make_async_copy(self.slots, self.slots, self.recv).wait()
                for h in range(2):
                    lo = self.base + h * self.size
                    rows = slice(lo, lo + self.size)
                    res = (
                        self.src[rows, :].astype(F32) + self.slots[h].astype(F32) + self.slots[2 + h].astype(F32))
                    if self.stage == 0:
                        t_v[self.j, self.d, rows, :] = res.astype(BF16)
                    else:
                        g_out[rows, :] = res

        def drain(self):
            @pl.when(jnp.logical_and(self.here, self.r > 0))
            def _():
                sent = self.slots.at[pl.ds(0, 2)]
                pltpu.make_async_copy(sent, sent, self.send).wait()

    def parts_of(j):
        return range(LAST_PARTS) if isinstance(j, int) and j == NZ - 1 else (None,)

    def trees(j, stage, parts=None):
        return [Tree(j, d, part, stage) for part in parts or parts_of(j) for d in range(2)]

    def combine(j):
        two = r0.at[pl.ds(0, 2)]
        pltpu.make_async_copy(two, two, p_recv.at[j]).wait()
        for d in range(2):
            ch = pair_chunk(j, d)
            mine = pb[ch, pl.ds(pl.multiple_of(core * PART, 16), PART), :].astype(F32)
            s_v[ch] = (mine + r0[ch].astype(F32)).astype(BF16)
        for t in trees(j, 0):
            t.begin()

    def second(j):
        for part in parts_of(j):
            for t in trees(j, 0, (part,)):
                t.finish()
            for t in trees(j, 1, (part,)):
                t.begin()

    def relay(j, stage):
        for t in trees(j, stage):
            t.relay()

    def last(j):
        for t in trees(j, 1):
            t.finish()

    def process(j):
        for d in range(2):
            ch = pair_chunk(j, d)

            def norm_tile(i, c):
                r = pl.ds(pl.multiple_of(i * TILE, TILE), TILE)
                gain = gain_ref[:, pl.ds(pl.multiple_of(ch * WIDTH, HD), WIDTH)]
                xs = xg[ch, r, :].astype(F32)
                n_v[d, r, :] = ((xs - mean_v[r, :]) * rstd_v[r, :] * gain).astype(BF16)
                return c

            lax.fori_loop(0, ROWS // TILE, norm_tile, 0)
            pb[ch] = dot(n_v[d], vr_b[...], 0, 0).astype(BF16)
            if d == 1:
                p_copy(j, 0).start()
        p_copy(j, 1).start()
        for d in range(2):
            ch = pair_chunk(j, d)
            vacc[...] += dot(n_v[d], w_v[pl.ds(pl.multiple_of(ch * WIDTH, HD), WIDTH), :], 1, 0)

    def early(j, carry):
        @pl.when(j >= 3)
        def _():
            arrival(j)

        process(j)

        @pl.when(j >= 1)
        def _():
            combine(j - 1)

        @pl.when(j >= 2)
        def _():
            relay(j - 2, 0)

        @pl.when(j >= 3)
        def _():
            second(j - 3)

        return carry

    lax.fori_loop(0, 4, early, 0)

    arrival(4)
    combine(3)
    relay(2, 0)
    second(1)
    process(4)
    relay(0, 1)
    relay(3, 0)
    relay(1, 1)

    def late(j, carry):
        arrival(j)
        combine(j - 1)

        @pl.when(j == 5)
        def _():
            second(2)
            last(0)
            last(1)

        second(j - 2)

        @pl.when(j >= 6)
        def _():
            last(j - 3)

        @pl.when(j == 6)
        def _():
            last(2)

        process(j)

        @pl.when(j == 5)
        def _():
            relay(2, 1)

        relay(j - 1, 0)
        relay(j - 2, 1)
        return carry

    lax.fori_loop(5, NZ, late, 0)

    def backward(h):
        cols = slice(h * HD, (h + 1) * HD)
        for t in range(tiles):
            r = slice(t * TILE, (t + 1) * TILE)
            lo = min(max(t * TILE - 64, 0), ROWS - SPAN)
            win = slice(lo, lo + SPAN)
            p = wts[h * tiles + t]
            dp_t = dot(vr_b[win, cols], cot_v[r, cols], 1, 1)
            centre = jnp.sum(p * dp_t, axis=0, keepdims=True)
            ds = (p * (dp_t - centre)).astype(BF16)
            dk_f[win, cols] += dot(ds, q_v[r, cols], 1, 0)
            dq_out[r, cols] = (dot(ds, k_v[win, cols], 0, 0) * scale).astype(BF16)

    vr_b[...] = vacc[...].astype(BF16)
    dk_f[...] = jnp.zeros_like(dk_f)
    combine(NZ - 1)
    second(NZ - 2)
    last(NZ - 3)
    backward(0)
    relay(NZ - 1, 0)
    relay(NZ - 2, 1)
    backward(1)
    second(NZ - 1)
    last(NZ - 2)
    backward(2)
    dk_out[...] = (dk_f[...] * scale).astype(BF16)
    stores = [
        pltpu.make_async_copy(dq_out, dq_hbm, local_sem.at[0]),
        pltpu.make_async_copy(dk_out, dk_hbm, local_sem.at[1]),
        pltpu.make_async_copy(g_out, g_hbm, local_sem.at[2]),
    ]
    stores[0].start()
    stores[1].start()

    def drain(j, carry):
        for stage in range(2):
            for t in trees(j, stage):
                t.drain()
        return carry

    relay(NZ - 1, 1)
    lax.fori_loop(0, NZ - 1, drain, 0)
    pltpu.make_async_copy(r0, r0, p_send).wait()
    last(NZ - 1)
    stores[2].start()
    drain(NZ - 1, 0)
    sent = xg.at[pl.ds(0, 2 * (NZ - 1))]
    pltpu.make_async_copy(sent, sent, ag_send).wait()
    pltpu.make_async_copy(some, some, cot_send).wait()
    pltpu.make_async_copy(first, first, st_send).wait()
    for store in stores:
        store.wait()


def hand_over(g_in, dq_in, dk_in, g_hbm, dq_hbm, dk_hbm, g_v, dq_v, dk_v, in_sem, out_sem):
    sides = ((g_in, g_v, g_hbm), (dq_in, dq_v, dq_hbm), (dk_in, dk_v, dk_hbm))
    inward = [pltpu.make_async_copy(a, v, in_sem.at[i]) for i, (a, v, o) in enumerate(sides)]
    outward = [pltpu.make_async_copy(v, o, out_sem.at[i]) for i, (a, v, o) in enumerate(sides)]
    for c in inward:
        c.start()
    for c, o in zip(inward, outward):
        c.wait()
        o.start()
    for o in outward:
        o.wait()


def body(
    patches, norm_gain, value_weight, queries, key_vectors, head_cotangent, image_owner, patch_count
):
    any_ = pl.BlockSpec(memory_space=pl.ANY)
    V, DMA = pltpu.VMEM, pltpu.SemaphoreType.DMA
    shapes = tuple(
        jax.ShapeDtypeStruct(shape, kind)
        for shape, kind in (((PART, WIDTH), F32), ((ROWS, WIDTH), BF16), ((ROWS, WIDTH), BF16)))
    done = pl.pallas_call(
        kernel,
        out_shape=shapes,
        in_specs=[any_] * 8,
        out_specs=(any_,) * 3,
        scratch_shapes=[
            V((1, NZ * 2 * WIDTH), F32),
            V((NDP, NDP), jnp.int32),
            V((NDP, NDP), jnp.int32),
            V((PART, WIDTH), F32),
            V((ROWS, WIDTH), BF16),
            V((ROWS, WIDTH), BF16),
            V((CHIPS, ROWS, WIDTH), BF16),
            V((NZ * 2 * WIDTH, WIDTH), BF16),
            V((ROWS, WIDTH), BF16),
            V((ROWS, WIDTH), BF16),
            V((NDP * CAP, WIDTH), BF16),
            V((ROWS, WIDTH), BF16),
            V((8, TILE), F32),
            V((NZ, 8, TILE), F32),
            V((ROWS, 1), F32),
            V((ROWS, 1), F32),
            V((ROWS, 1), F32),
            V((ROWS, 1), F32),
            V((8, ROWS), F32),
            V((3 * ROWS // TILE, SPAN, TILE), F32),
            V((ROWS, WIDTH), F32),
            V((ROWS, WIDTH), BF16),
            V((ROWS, WIDTH), F32),
            V((2, ROWS, WIDTH), BF16),
            V((CHIPS, 2 * PART, WIDTH), BF16),
            V((CHIPS, PART, WIDTH), BF16),
            V((CHIPS, PART, WIDTH), BF16),
            V((ROWS, WIDTH), F32),
            V((NZ, 2, PART, WIDTH), BF16),
            V((NZ - 1, 2, 2, 4, PART // 2, WIDTH), BF16),
            DMA((9,)), DMA, DMA((2, 7)), DMA, DMA, DMA, DMA, DMA, DMA((NZ,)),
            DMA((NZ - 1, 2, 2)), DMA((NZ - 1, 2, 2)),
            V((2, LAST_PARTS, 2, 4, PART // LAST_PARTS // 2, WIDTH), BF16),
            DMA((2, LAST_PARTS, 2)), DMA((2, LAST_PARTS, 2)),
        ],
        compiler_params=pltpu.CompilerParams(
            collective_id=0, has_side_effects=True, vmem_limit_bytes=60 * 1024 * 1024
        ),
    )(
        patches, norm_gain.reshape(1, -1), value_weight, queries, key_vectors, head_cotangent,
        image_owner, patch_count,
    )
    return pl.pallas_call(
        hand_over,
        out_shape=shapes,
        in_specs=[any_] * 3,
        out_specs=(any_,) * 3,
        scratch_shapes=[V(s.shape, s.dtype) for s in shapes] + [DMA((3,)), DMA((3,))],
    )(*done)


def solution(mesh):
    return jax.shard_map(
        body,
        mesh=mesh,
        in_specs=(
            P("dp", "mp"), P(), P(None, "mp"), P("dp", "mp"), P("dp", "mp"), P("dp", "mp"), P(), P(),
        ),
        out_specs=(P("dp", "mp"), P("dp", "mp"), P("dp", "mp")),
        check_vma=False,
    )
```

```python
import jax
import jax.numpy as jnp
from jax import lax
from jax.experimental import pallas as pl
from jax.experimental.pallas import tpu as pltpu
from jax.sharding import PartitionSpec as P

HD = 128
MESH = pl.DeviceIdType.MESH
F32 = jnp.float32
BF16 = jnp.bfloat16
SIDE = 4
NZ = 8
NDP = 32
CHIPS = 16
ROWS = 512
CAP = 32
WIDTH = 384
PART = 192
TILE = 128
SPAN = 256
LAST_PARTS = 3


def iota(shape, dim):
    return lax.broadcasted_iota(jnp.int32, shape, dim)


def dot(a, b, da, db):
    return lax.dot_general(a, b, (((da,), (db,)), ((), ())), preferred_element_type=F32)


def window(t):
    return jnp.clip(t * TILE - 64, 0, ROWS - SPAN)


def kernel(
    x_hbm, gain_hbm, w_hbm, q_hbm, k_hbm, hc_hbm, owner_hbm, count_hbm,
    g_hbm, dq_hbm, dk_hbm,
    gain_ref, owner_ref, count_ref, g_out, dq_out, dk_out,
    xg, w_v, q_v, k_v, cotr, cot_v, stat_src, stats, mean_v, rstd_v, idx_v, segc_v, segr_v,
    wts, vr_f, vr_b, vacc, n_v, pb, r0, s_v, dk_f, t_v, tree,
    local_sem, ag_send, ag_recv, cot_send, cot_recv, st_send, st_recv, p_send, p_recv,
    rs_send, rs_recv, end_tree, end_send, end_recv,
):
    dp = lax.axis_index("dp")
    z = lax.axis_index("mp")
    core = lax.rem(dp, 2)
    chip = dp // 2
    px = chip // SIDE
    py = lax.rem(chip, SIDE)
    sibling = chip * 2 + 1 - core

    loads = [
        pltpu.make_async_copy(x_hbm.at[:, pl.ds(h * WIDTH, WIDTH)], xg.at[2 * z + h], local_sem.at[h])
        for h in range(2)
    ]
    loads += [
        pltpu.make_async_copy(q_hbm, q_v, local_sem.at[2]),
        pltpu.make_async_copy(k_hbm, k_v, local_sem.at[3]),
        pltpu.make_async_copy(w_hbm, w_v, local_sem.at[4]),
        pltpu.make_async_copy(
            hc_hbm.at[pl.ds(pl.multiple_of(dp * CAP, CAP), CAP)],
            cotr.at[pl.ds(pl.multiple_of(dp * CAP, CAP), CAP)], local_sem.at[5]),
        pltpu.make_async_copy(owner_hbm, owner_ref, local_sem.at[6]),
        pltpu.make_async_copy(count_hbm, count_ref, local_sem.at[7]),
        pltpu.make_async_copy(gain_hbm, gain_ref, local_sem.at[8]),
    ]
    barrier = pltpu.get_barrier_semaphore()

    def greet_dp(j, carry):
        pl.semaphore_signal(barrier, inc=1, device_id={"dp": lax.rem(dp + j, NDP)}, device_id_type=MESH)
        return carry

    lax.fori_loop(1, NDP, greet_dp, 0)

    def greet_z(j, carry):
        pl.semaphore_signal(barrier, inc=1, device_id={"mp": lax.rem(z + j, NZ)}, device_id_type=MESH)
        return carry

    lax.fori_loop(1, NZ, greet_z, 0)
    for load in loads:
        load.start()
    pl.semaphore_wait(barrier, NDP - 1 + NZ - 1)

    def pair_chunk(j, d):
        origin = lax.rem(z + NZ + (2 * d - 1) * ((j + 1) // 2), NZ)
        return origin * 2 + lax.rem(j + 1 + d, 2)

    def next_z(d):
        return lax.rem(z + NZ + 1 - 2 * d, NZ)

    def ag_copy(d, e, src):
        origin = lax.rem(z + NZ + (2 * d - 1) * (e // 2), NZ)
        ch = origin * 2 + lax.rem(e + d, 2)
        return pltpu.make_async_remote_copy(
            src_ref=xg.at[ch] if src is None else src, dst_ref=xg.at[ch],
            send_sem=ag_send, recv_sem=ag_recv.at[d, e],
            device_id={"mp": next_z(d)}, device_id_type=MESH)

    for d in range(2):
        ag_copy(d, 0, x_hbm.at[:, pl.ds(d * WIDTH, WIDTH)]).start()

    def cot_copy(j):
        to = lax.rem(dp + j, NDP)
        return pltpu.make_async_remote_copy(
            src_ref=hc_hbm.at[pl.ds(pl.multiple_of(to * CAP, CAP), CAP)],
            dst_ref=cotr.at[pl.ds(pl.multiple_of(dp * CAP, CAP), CAP)],
            send_sem=cot_send, recv_sem=cot_recv, device_id={"dp": to}, device_id_type=MESH)

    def start_cot(j, carry):
        cot_copy(j).start()
        return carry

    lax.fori_loop(1, NDP, start_cot, 0)

    loads[0].wait()
    loads[1].wait()
    width = 2 * WIDTH
    tiles = ROWS // TILE

    def stat_tile(i, carry):
        r = pl.ds(pl.multiple_of(i * TILE, TILE), TILE)
        xa = xg[2 * z, r, :].astype(F32)
        xb = xg[2 * z + 1, r, :].astype(F32)
        m = (jnp.sum(xa, axis=1, keepdims=True) + jnp.sum(xb, axis=1, keepdims=True)) / width
        xa = xa - m
        xb = xb - m
        m2 = jnp.sum(xa * xa, axis=1, keepdims=True) + jnp.sum(xb * xb, axis=1, keepdims=True)
        lane = iota((TILE, TILE), 1)
        both = jnp.where(lane == 0, m, jnp.where(lane == 1, m2, 0.0)).T
        stat_src[pl.ds(i, 1), :] = both[0:1, :]
        stat_src[pl.ds(tiles + i, 1), :] = both[1:2, :]
        return carry

    lax.fori_loop(0, ROWS // TILE, stat_tile, 0)

    loads[6].wait()
    loads[7].wait()

    row32 = iota((NDP, NDP), 0)
    col32 = iota((NDP, NDP), 1)
    mine = row32 == dp
    own_l = jnp.sum(jnp.where(mine, owner_ref[...].astype(F32), 0.0), axis=0, keepdims=True)
    cnt_l = jnp.sum(jnp.where(mine, count_ref[...].astype(F32), 0.0), axis=0, keepdims=True)
    cnt_s = jnp.sum(jnp.where(row32 == col32, cnt_l, 0.0), axis=1, keepdims=True)
    ends_l = jnp.sum(jnp.where(row32 <= col32, cnt_s, 0.0), axis=0, keepdims=True)
    ends_s = jnp.sum(jnp.where(col32 <= row32, cnt_l, 0.0), axis=1, keepdims=True)
    starts_l = ends_l - cnt_l
    row = iota((ROWS, NDP), 0).astype(F32)
    image = jnp.sum(jnp.where(ends_l <= row, 1.0, 0.0), axis=1, keepdims=True)
    picked = iota((ROWS, NDP), 1).astype(F32) == image
    row_owner = jnp.sum(jnp.where(picked, own_l, 0.0), axis=1, keepdims=True)
    row_start = jnp.sum(jnp.where(picked, starts_l, 0.0), axis=1, keepdims=True)
    idx_v[...] = row_owner * CAP + row[:, 0:1] - row_start
    segc_v[...] = image
    lane_row = iota((NDP, ROWS), 1).astype(F32)
    segr_v[...] = jnp.broadcast_to(
        jnp.sum(jnp.where(ends_s <= lane_row, 1.0, 0.0), axis=0, keepdims=True), (8, ROWS))

    def stat_copy(j):
        return pltpu.make_async_remote_copy(
            src_ref=stat_src, dst_ref=stats.at[z], send_sem=st_send, recv_sem=st_recv,
            device_id={"mp": lax.rem(z + j, NZ)}, device_id_type=MESH)

    def start_stat(j, carry):
        stat_copy(j).start()
        return carry

    lax.fori_loop(1, NZ, start_stat, 0)
    for d in range(2):
        ag_copy(d, 1, x_hbm.at[:, pl.ds((1 - d) * WIDTH, WIDTH)]).start()

    def arrival(j):
        for d in range(2):
            ch = pair_chunk(j, d)
            pltpu.make_async_remote_copy(
                src_ref=xg.at[ch], dst_ref=xg.at[ch], send_sem=ag_send,
                recv_sem=ag_recv.at[d, j - 1], device_id={"mp": next_z(d)}, device_id_type=MESH).wait_recv()

            def forward():
                ag_copy(d, j + 1, None).start()

            if isinstance(j, int):
                if j <= NZ - 3:
                    forward()
            else:
                pl.when(j <= NZ - 3)(forward)

    arrival(1)

    loads[2].wait()
    loads[3].wait()
    loads[5].wait()
    some = cotr.at[pl.ds(0, (NDP - 1) * CAP)]
    pltpu.make_async_copy(some, some, cot_recv).wait()

    def gather_tile(i, carry):
        r = pl.ds(pl.multiple_of(i * TILE, TILE), TILE)
        lane = iota((TILE, NDP * CAP), 1).astype(F32)
        onehot = jnp.where(lane == idx_v[r, :], 1.0, 0.0).astype(BF16)
        cot_v[r, :] = dot(onehot, cotr[...], 1, 0).astype(BF16)
        return carry

    lax.fori_loop(0, ROWS // TILE, gather_tile, 0)
    vr_f[...] = jnp.zeros_like(vr_f)
    vacc[...] = jnp.zeros_like(vacc)
    scale = HD ** (-0.5)
    heads = WIDTH // HD

    def forward(i, carry):
        h = i // tiles
        t = lax.rem(i, tiles)
        cols = pl.ds(pl.multiple_of(h * HD, HD), HD)
        r = pl.ds(pl.multiple_of(t * TILE, TILE), TILE)
        win = pl.ds(pl.multiple_of(window(t), 64), SPAN)
        st = dot(k_v[win, cols], q_v[r, cols], 1, 1) * scale
        st = jnp.where(segc_v[win, :] == segr_v[0:1, r], st, -1e9)
        e = jnp.exp(st - jnp.max(st, axis=0, keepdims=True))
        p = e / jnp.sum(e, axis=0, keepdims=True)
        wts[i] = p
        vr_f[win, cols] += dot(p.astype(BF16), cot_v[r, cols], 1, 0)
        return carry

    lax.fori_loop(0, heads * tiles, forward, 0)
    vr_b[...] = vr_f[...].astype(BF16)
    arrival(2)

    first = stats.at[pl.ds(0, NZ - 1)]
    pltpu.make_async_copy(first, first, st_recv).wait()
    stats[z] = stat_src[...]
    mean = sum(stats[i, 0:tiles, :] for i in range(NZ)) / NZ
    m2 = sum(stats[i, tiles:8, :] + width * (stats[i, 0:tiles, :] - mean) ** 2 for i in range(NZ))
    rstd = lax.rsqrt(m2 / (width * NZ) + 1e-06)
    sub = iota((TILE, TILE), 0)
    for i in range(tiles):
        r = slice(i * TILE, (i + 1) * TILE)
        both = jnp.where(sub == 0, mean[i:i + 1, :], jnp.where(sub == 1, rstd[i:i + 1, :], 0.0)).T
        mean_v[r, :] = both[:, 0:1]
        rstd_v[r, :] = both[:, 1:2]
    loads[4].wait()
    loads[8].wait()

    def p_copy(j, d):
        ch = pair_chunk(j, d)
        return pltpu.make_async_remote_copy(
            src_ref=pb.at[ch, pl.ds(pl.multiple_of((1 - core) * PART, 16), PART)], dst_ref=r0.at[ch],
            send_sem=p_send, recv_sem=p_recv.at[j],
            device_id={"dp": sibling}, device_id_type=MESH)

    def at_pos(axis, off):
        if axis == 0:
            return (lax.rem(px + SIDE + off, SIDE) * SIDE + py) * 2 + core
        return (px * SIDE + lax.rem(py + SIDE + off, SIDE)) * 2 + core

    class Tree:
        def __init__(self, j, d, part, stage):
            self.j, self.d, self.stage = j, d, stage
            if part is None:
                self.base, self.size = 0, PART // 2
                self.slots, self.send, self.recv = tree.at[j, d, stage], rs_send.at[j, d], rs_recv.at[j, d, stage]
            else:
                self.size = PART // LAST_PARTS // 2
                self.base = part * 2 * self.size
                self.slots = end_tree.at[d, part, stage]
                self.send, self.recv = end_send.at[d, part], end_recv.at[d, part, stage]
            ch = pair_chunk(j, d)
            self.axis = 1 - d if stage == 0 else d
            place, goal = (px, py), (ch // SIDE, lax.rem(ch, SIDE))
            self.keeps = chip == ch
            self.r = lax.rem(place[self.axis] + SIDE - goal[self.axis], SIDE)
            self.here = place[1 - self.axis] == goal[1 - self.axis] if stage else px >= 0
            self.src = s_v.at[ch] if stage == 0 else t_v.at[j, d]
            self.low = self.r // 2
            self.sgn = 2 * self.low - 1

        def half(self, h):
            return pl.ds(pl.multiple_of(self.base + h * self.size, 16), self.size)

        def copy(self, src, off, slot):
            return pltpu.make_async_remote_copy(
                src_ref=src, dst_ref=self.slots.at[slot], send_sem=self.send, recv_sem=self.recv,
                device_id={"dp": at_pos(self.axis, off)}, device_id_type=MESH)

        def is_far(self):
            return jnp.logical_and(self.here, self.r == 2)

        def is_near(self):
            return jnp.logical_and(self.here, lax.rem(self.r, 2) == 1)

        def is_goal(self):
            return jnp.logical_and(self.here, self.r == 0)

        def far(self):
            return [self.copy(self.src.at[self.half(0)], -1, 0), self.copy(self.src.at[self.half(1)], 1, 0)]

        def raw(self):
            return self.copy(self.src.at[self.half(1 - self.low)], self.sgn, 1 + self.low)

        def total(self):
            return self.copy(self.slots.at[1], self.sgn, 3 * self.low)

        def begin(self):
            @pl.when(self.is_far())
            def _():
                for c in self.far():
                    c.start()

            @pl.when(self.is_near())
            def _():
                self.raw().start()

        def relay(self):
            @pl.when(self.is_near())
            def _():
                self.copy(self.slots.at[0], 1, 0).wait_recv()
                self.slots[1] = (self.slots[0].astype(F32) + self.src[self.half(self.low), :].astype(F32)).astype(BF16)
                self.total().start()

        def finish(self):
            @pl.when(self.is_goal())
            def _():
                pltpu.make_async_copy(self.slots, self.slots, self.recv).wait()
                for h in range(2):
                    lo = self.base + h * self.size
                    rows = slice(lo, lo + self.size)
                    res = (
                        self.src[rows, :].astype(F32) + self.slots[h].astype(F32) + self.slots[2 + h].astype(F32))
                    if self.stage == 0:
                        t_v[self.j, self.d, rows, :] = res.astype(BF16)
                    else:
                        g_out[rows, :] = res

        def drain(self):
            @pl.when(jnp.logical_not(self.keeps))
            def _():
                sent = self.slots.at[pl.ds(0, 2)]
                pltpu.make_async_copy(sent, sent, self.send).wait()

    def parts_of(j):
        return range(LAST_PARTS) if isinstance(j, int) and j == NZ - 1 else (None,)

    def trees(j, stage, parts=None):
        return [Tree(j, d, part, stage) for part in parts or parts_of(j) for d in range(2)]

    def combine(j):
        two = r0.at[pl.ds(0, 2)]
        pltpu.make_async_copy(two, two, p_recv.at[j]).wait()
        for d in range(2):
            ch = pair_chunk(j, d)
            mine = pb[ch, pl.ds(pl.multiple_of(core * PART, 16), PART), :].astype(F32)
            s_v[ch] = (mine + r0[ch].astype(F32)).astype(BF16)
        for t in trees(j, 0):
            t.begin()

    def second(j):
        for part in parts_of(j):
            for t in trees(j, 0, (part,)):
                t.finish()
            for t in trees(j, 1, (part,)):
                t.begin()

    def relay(j, stage):
        for t in trees(j, stage):
            t.relay()

    def last(j):
        for t in trees(j, 1):
            t.finish()

    def process(j):
        for d in range(2):
            ch = pair_chunk(j, d)

            def norm_tile(i, c):
                r = pl.ds(pl.multiple_of(i * TILE, TILE), TILE)
                gain = gain_ref[:, pl.ds(pl.multiple_of(ch * WIDTH, HD), WIDTH)]
                xs = xg[ch, r, :].astype(F32)
                n_v[d, r, :] = ((xs - mean_v[r, :]) * rstd_v[r, :] * gain).astype(BF16)
                return c

            lax.fori_loop(0, ROWS // TILE, norm_tile, 0)
            pb[ch] = dot(n_v[d], vr_b[...], 0, 0).astype(BF16)
            if d == 1:
                p_copy(j, 0).start()
        p_copy(j, 1).start()
        for d in range(2):
            ch = pair_chunk(j, d)
            vacc[...] += dot(n_v[d], w_v[pl.ds(pl.multiple_of(ch * WIDTH, HD), WIDTH), :], 1, 0)

    def early(j, carry):
        @pl.when(j >= 3)
        def _():
            arrival(j)

        process(j)

        @pl.when(j >= 1)
        def _():
            combine(j - 1)

        @pl.when(j >= 2)
        def _():
            relay(j - 2, 0)

        @pl.when(j >= 3)
        def _():
            second(j - 3)

        return carry

    lax.fori_loop(0, 4, early, 0)

    arrival(4)
    combine(3)
    relay(2, 0)
    second(1)
    process(4)
    combine(4)
    relay(0, 1)
    relay(3, 0)
    second(2)
    relay(1, 1)
    arrival(5)
    relay(4, 0)
    second(3)
    relay(2, 1)
    last(0)
    last(1)
    process(5)
    combine(5)
    second(4)
    relay(3, 1)
    last(2)
    arrival(6)
    relay(5, 0)
    relay(4, 1)
    process(6)
    combine(6)
    second(5)
    last(3)
    last(4)
    arrival(7)
    relay(6, 0)
    relay(5, 1)
    process(7)

    def backward(h):
        cols = slice(h * HD, (h + 1) * HD)
        for t in range(tiles):
            r = slice(t * TILE, (t + 1) * TILE)
            lo = min(max(t * TILE - 64, 0), ROWS - SPAN)
            win = slice(lo, lo + SPAN)
            p = wts[h * tiles + t]
            dp_t = dot(vr_b[win, cols], cot_v[r, cols], 1, 1)
            centre = jnp.sum(p * dp_t, axis=0, keepdims=True)
            ds = (p * (dp_t - centre)).astype(BF16)
            dk_f[win, cols] += dot(ds, q_v[r, cols], 1, 0)
            dq_out[r, cols] = (dot(ds, k_v[win, cols], 0, 0) * scale).astype(BF16)

    vr_b[...] = vacc[...].astype(BF16)
    dk_f[...] = jnp.zeros_like(dk_f)
    combine(NZ - 1)
    second(NZ - 2)
    relay(NZ - 1, 0)
    last(NZ - 3)
    relay(NZ - 2, 1)
    backward(0)
    backward(1)
    second(NZ - 1)
    relay(NZ - 1, 1)
    last(NZ - 2)
    backward(2)
    dk_out[...] = (dk_f[...] * scale).astype(BF16)
    stores = [
        pltpu.make_async_copy(dq_out, dq_hbm, local_sem.at[0]),
        pltpu.make_async_copy(dk_out, dk_hbm, local_sem.at[1]),
        pltpu.make_async_copy(g_out, g_hbm, local_sem.at[2]),
    ]
    stores[0].start()
    stores[1].start()

    def drain(j, carry):
        for t in trees(j, 0):
            t.drain()
        return carry

    lax.fori_loop(0, NZ - 1, drain, 0)
    pltpu.make_async_copy(r0, r0, p_send).wait()
    last(NZ - 1)
    stores[2].start()
    drain(NZ - 1, 0)
    sent = xg.at[pl.ds(0, 2 * (NZ - 1))]
    pltpu.make_async_copy(sent, sent, ag_send).wait()
    pltpu.make_async_copy(some, some, cot_send).wait()
    pltpu.make_async_copy(first, first, st_send).wait()
    for store in stores:
        store.wait()


def hand_over(g_in, dq_in, dk_in, g_hbm, dq_hbm, dk_hbm, sem):
    copies = [
        pltpu.make_async_copy(a, o, sem.at[i])
        for i, (a, o) in enumerate(((g_in, g_hbm), (dq_in, dq_hbm), (dk_in, dk_hbm)))
    ]
    for c in copies:
        c.start()
    for c in copies:
        c.wait()


def body(
    patches, norm_gain, value_weight, queries, key_vectors, head_cotangent, image_owner, patch_count
):
    any_ = pl.BlockSpec(memory_space=pl.ANY)
    V, DMA = pltpu.VMEM, pltpu.SemaphoreType.DMA
    shapes = tuple(
        jax.ShapeDtypeStruct(shape, kind)
        for shape, kind in (((PART, WIDTH), F32), ((ROWS, WIDTH), BF16), ((ROWS, WIDTH), BF16)))
    done = pl.pallas_call(
        kernel,
        out_shape=shapes,
        in_specs=[any_] * 8,
        out_specs=(any_,) * 3,
        scratch_shapes=[
            V((1, NZ * 2 * WIDTH), F32),
            V((NDP, NDP), jnp.int32),
            V((NDP, NDP), jnp.int32),
            V((PART, WIDTH), F32),
            V((ROWS, WIDTH), BF16),
            V((ROWS, WIDTH), BF16),
            V((CHIPS, ROWS, WIDTH), BF16),
            V((NZ * 2 * WIDTH, WIDTH), BF16),
            V((ROWS, WIDTH), BF16),
            V((ROWS, WIDTH), BF16),
            V((NDP * CAP, WIDTH), BF16),
            V((ROWS, WIDTH), BF16),
            V((8, TILE), F32),
            V((NZ, 8, TILE), F32),
            V((ROWS, 1), F32),
            V((ROWS, 1), F32),
            V((ROWS, 1), F32),
            V((ROWS, 1), F32),
            V((8, ROWS), F32),
            V((3 * ROWS // TILE, SPAN, TILE), F32),
            V((ROWS, WIDTH), F32),
            V((ROWS, WIDTH), BF16),
            V((ROWS, WIDTH), F32),
            V((2, ROWS, WIDTH), BF16),
            V((CHIPS, 2 * PART, WIDTH), BF16),
            V((CHIPS, PART, WIDTH), BF16),
            V((CHIPS, PART, WIDTH), BF16),
            V((ROWS, WIDTH), F32),
            V((NZ, 2, PART, WIDTH), BF16),
            V((NZ - 1, 2, 2, 4, PART // 2, WIDTH), BF16),
            DMA((9,)), DMA, DMA((2, 7)), DMA, DMA, DMA, DMA, DMA, DMA((NZ,)),
            DMA((NZ - 1, 2)), DMA((NZ - 1, 2, 2)),
            V((2, LAST_PARTS, 2, 4, PART // LAST_PARTS // 2, WIDTH), BF16),
            DMA((2, LAST_PARTS)), DMA((2, LAST_PARTS, 2)),
        ],
        compiler_params=pltpu.CompilerParams(
            collective_id=0, has_side_effects=True, vmem_limit_bytes=50 * 1024 * 1024
        ),
    )(
        *(
            pltpu.with_memory_space_constraint(a, pltpu.HBM)
            for a in (
                patches, norm_gain.reshape(1, -1), value_weight, queries, key_vectors, head_cotangent,
                image_owner, patch_count,
            )
        )
    )
    return pl.pallas_call(
        hand_over,
        out_shape=shapes,
        in_specs=[pl.BlockSpec(memory_space=pltpu.VMEM)] * 3,
        out_specs=(any_,) * 3,
        scratch_shapes=[DMA((3,))],
        compiler_params=pltpu.CompilerParams(vmem_limit_bytes=4 * 1024 * 1024),
    )(*done)


def solution(mesh):
    return jax.shard_map(
        body,
        mesh=mesh,
        in_specs=(
            P("dp", "mp"), P(), P(None, "mp"), P("dp", "mp"), P("dp", "mp"), P("dp", "mp"), P(), P(),
        ),
        out_specs=(P("dp", "mp"), P("dp", "mp"), P("dp", "mp")),
        check_vma=False,
    )
```

```python
import jax
import jax.numpy as jnp
from jax import lax
from jax.experimental import pallas as pl
from jax.experimental.pallas import tpu as pltpu
from jax.sharding import PartitionSpec as P

HD = 128
MESH = pl.DeviceIdType.MESH
F32 = jnp.float32
BF16 = jnp.bfloat16
SIDE = 4
NZ = 8
NDP = 32
CHIPS = 16
ROWS = 512
CAP = 32
WIDTH = 384
PART = 192
TILE = 128
SPAN = 256
LAST_PARTS = 3


def iota(shape, dim):
    return lax.broadcasted_iota(jnp.int32, shape, dim)


def dot(a, b, da, db):
    return lax.dot_general(a, b, (((da,), (db,)), ((), ())), preferred_element_type=F32)


def window(t):
    return jnp.clip(t * TILE - 64, 0, ROWS - SPAN)


def kernel(
    x_hbm, gain_hbm, w_hbm, q_hbm, k_hbm, hc_hbm, owner_hbm, count_hbm,
    g_hbm, dq_hbm, dk_hbm,
    gain_ref, owner_ref, count_ref, g_out, dq_out, dk_out,
    xg, w_v, q_v, k_v, cotr, cot_v, stat_src, stats, mean_v, rstd_v, idx_v, segc_v, segr_v,
    wts, vr_f, vr_b, vacc, n_v, pb, r0, s_v, dk_f, t_v, tree,
    local_sem, ag_send, ag_recv, cot_send, cot_recv, st_send, st_recv, p_send, p_recv,
    rs_send, rs_recv, end_tree, end_send, end_recv,
):
    dp = lax.axis_index("dp")
    z = lax.axis_index("mp")
    core = lax.rem(dp, 2)
    chip = dp // 2
    px = chip // SIDE
    py = lax.rem(chip, SIDE)
    sibling = chip * 2 + 1 - core

    loads = [
        pltpu.make_async_copy(x_hbm.at[:, pl.ds(h * WIDTH, WIDTH)], xg.at[2 * z + h], local_sem.at[h])
        for h in range(2)
    ]
    loads += [
        pltpu.make_async_copy(q_hbm, q_v, local_sem.at[2]),
        pltpu.make_async_copy(k_hbm, k_v, local_sem.at[3]),
        pltpu.make_async_copy(w_hbm, w_v, local_sem.at[4]),
        pltpu.make_async_copy(
            hc_hbm.at[pl.ds(pl.multiple_of(dp * CAP, CAP), CAP)],
            cotr.at[pl.ds(pl.multiple_of(dp * CAP, CAP), CAP)], local_sem.at[5]),
        pltpu.make_async_copy(owner_hbm, owner_ref, local_sem.at[6]),
        pltpu.make_async_copy(count_hbm, count_ref, local_sem.at[7]),
        pltpu.make_async_copy(gain_hbm, gain_ref, local_sem.at[8]),
    ]
    barrier = pltpu.get_barrier_semaphore()

    def greet_dp(j, carry):
        pl.semaphore_signal(barrier, inc=1, device_id={"dp": lax.rem(dp + j, NDP)}, device_id_type=MESH)
        return carry

    lax.fori_loop(1, NDP, greet_dp, 0)

    def greet_z(j, carry):
        pl.semaphore_signal(barrier, inc=1, device_id={"mp": lax.rem(z + j, NZ)}, device_id_type=MESH)
        return carry

    lax.fori_loop(1, NZ, greet_z, 0)
    for load in loads:
        load.start()
    pl.semaphore_wait(barrier, NDP - 1 + NZ - 1)

    def pair_chunk(j, d):
        origin = lax.rem(z + NZ + (2 * d - 1) * ((j + 1) // 2), NZ)
        return origin * 2 + lax.rem(j + 1 + d, 2)

    def next_z(d):
        return lax.rem(z + NZ + 1 - 2 * d, NZ)

    def ag_copy(d, e, src):
        origin = lax.rem(z + NZ + (2 * d - 1) * (e // 2), NZ)
        ch = origin * 2 + lax.rem(e + d, 2)
        return pltpu.make_async_remote_copy(
            src_ref=xg.at[ch] if src is None else src, dst_ref=xg.at[ch],
            send_sem=ag_send, recv_sem=ag_recv.at[d, e],
            device_id={"mp": next_z(d)}, device_id_type=MESH)

    for d in range(2):
        ag_copy(d, 0, x_hbm.at[:, pl.ds(d * WIDTH, WIDTH)]).start()

    def cot_copy(j):
        to = lax.rem(dp + j, NDP)
        return pltpu.make_async_remote_copy(
            src_ref=hc_hbm.at[pl.ds(pl.multiple_of(to * CAP, CAP), CAP)],
            dst_ref=cotr.at[pl.ds(pl.multiple_of(dp * CAP, CAP), CAP)],
            send_sem=cot_send, recv_sem=cot_recv, device_id={"dp": to}, device_id_type=MESH)

    def start_cot(j, carry):
        cot_copy(j).start()
        return carry

    lax.fori_loop(1, NDP, start_cot, 0)

    loads[0].wait()
    loads[1].wait()
    width = 2 * WIDTH
    tiles = ROWS // TILE

    def stat_tile(i, carry):
        r = pl.ds(pl.multiple_of(i * TILE, TILE), TILE)
        xa = xg[2 * z, r, :].astype(F32)
        xb = xg[2 * z + 1, r, :].astype(F32)
        m = (jnp.sum(xa, axis=1, keepdims=True) + jnp.sum(xb, axis=1, keepdims=True)) / width
        xa = xa - m
        xb = xb - m
        m2 = jnp.sum(xa * xa, axis=1, keepdims=True) + jnp.sum(xb * xb, axis=1, keepdims=True)
        lane = iota((TILE, TILE), 1)
        both = jnp.where(lane == 0, m, jnp.where(lane == 1, m2, 0.0)).T
        stat_src[pl.ds(i, 1), :] = both[0:1, :]
        stat_src[pl.ds(tiles + i, 1), :] = both[1:2, :]
        return carry

    lax.fori_loop(0, ROWS // TILE, stat_tile, 0)

    loads[6].wait()
    loads[7].wait()

    row32 = iota((NDP, NDP), 0)
    col32 = iota((NDP, NDP), 1)
    mine = row32 == dp
    own_l = jnp.sum(jnp.where(mine, owner_ref[...].astype(F32), 0.0), axis=0, keepdims=True)
    cnt_l = jnp.sum(jnp.where(mine, count_ref[...].astype(F32), 0.0), axis=0, keepdims=True)
    cnt_s = jnp.sum(jnp.where(row32 == col32, cnt_l, 0.0), axis=1, keepdims=True)
    ends_l = jnp.sum(jnp.where(row32 <= col32, cnt_s, 0.0), axis=0, keepdims=True)
    ends_s = jnp.sum(jnp.where(col32 <= row32, cnt_l, 0.0), axis=1, keepdims=True)
    starts_l = ends_l - cnt_l
    row = iota((ROWS, NDP), 0).astype(F32)
    image = jnp.sum(jnp.where(ends_l <= row, 1.0, 0.0), axis=1, keepdims=True)
    picked = iota((ROWS, NDP), 1).astype(F32) == image
    row_owner = jnp.sum(jnp.where(picked, own_l, 0.0), axis=1, keepdims=True)
    row_start = jnp.sum(jnp.where(picked, starts_l, 0.0), axis=1, keepdims=True)
    idx_v[...] = row_owner * CAP + row[:, 0:1] - row_start
    segc_v[...] = image
    lane_row = iota((NDP, ROWS), 1).astype(F32)
    segr_v[...] = jnp.broadcast_to(
        jnp.sum(jnp.where(ends_s <= lane_row, 1.0, 0.0), axis=0, keepdims=True), (8, ROWS))

    def stat_copy(j):
        return pltpu.make_async_remote_copy(
            src_ref=stat_src, dst_ref=stats.at[z], send_sem=st_send, recv_sem=st_recv,
            device_id={"mp": lax.rem(z + j, NZ)}, device_id_type=MESH)

    def start_stat(j, carry):
        stat_copy(j).start()
        return carry

    lax.fori_loop(1, NZ, start_stat, 0)
    for d in range(2):
        ag_copy(d, 1, x_hbm.at[:, pl.ds((1 - d) * WIDTH, WIDTH)]).start()

    def arrival(j):
        for d in range(2):
            ch = pair_chunk(j, d)
            pltpu.make_async_remote_copy(
                src_ref=xg.at[ch], dst_ref=xg.at[ch], send_sem=ag_send,
                recv_sem=ag_recv.at[d, j - 1], device_id={"mp": next_z(d)}, device_id_type=MESH).wait_recv()

            def forward():
                ag_copy(d, j + 1, None).start()

            if isinstance(j, int):
                if j <= NZ - 3:
                    forward()
            else:
                pl.when(j <= NZ - 3)(forward)

    arrival(1)

    loads[2].wait()
    loads[3].wait()
    loads[5].wait()
    some = cotr.at[pl.ds(0, (NDP - 1) * CAP)]
    pltpu.make_async_copy(some, some, cot_recv).wait()

    def gather_tile(i, carry):
        r = pl.ds(pl.multiple_of(i * TILE, TILE), TILE)
        lane = iota((TILE, NDP * CAP), 1).astype(F32)
        onehot = jnp.where(lane == idx_v[r, :], 1.0, 0.0).astype(BF16)
        cot_v[r, :] = dot(onehot, cotr[...], 1, 0).astype(BF16)
        return carry

    lax.fori_loop(0, ROWS // TILE, gather_tile, 0)
    vr_f[...] = jnp.zeros_like(vr_f)
    vacc[...] = jnp.zeros_like(vacc)
    scale = HD ** (-0.5)
    heads = WIDTH // HD

    def forward(i, carry):
        h = i // tiles
        t = lax.rem(i, tiles)
        cols = pl.ds(pl.multiple_of(h * HD, HD), HD)
        r = pl.ds(pl.multiple_of(t * TILE, TILE), TILE)
        win = pl.ds(pl.multiple_of(window(t), 64), SPAN)
        st = dot(k_v[win, cols], q_v[r, cols], 1, 1) * scale
        st = jnp.where(segc_v[win, :] == segr_v[0:1, r], st, -1e9)
        e = jnp.exp(st - jnp.max(st, axis=0, keepdims=True))
        p = e / jnp.sum(e, axis=0, keepdims=True)
        wts[i] = p
        vr_f[win, cols] += dot(p.astype(BF16), cot_v[r, cols], 1, 0)
        return carry

    lax.fori_loop(0, heads * tiles, forward, 0)
    vr_b[...] = vr_f[...].astype(BF16)
    arrival(2)

    first = stats.at[pl.ds(0, NZ - 1)]
    pltpu.make_async_copy(first, first, st_recv).wait()
    stats[z] = stat_src[...]
    mean = sum(stats[i, 0:tiles, :] for i in range(NZ)) / NZ
    m2 = sum(stats[i, tiles:8, :] + width * (stats[i, 0:tiles, :] - mean) ** 2 for i in range(NZ))
    rstd = lax.rsqrt(m2 / (width * NZ) + 1e-06)
    sub = iota((TILE, TILE), 0)
    for i in range(tiles):
        r = slice(i * TILE, (i + 1) * TILE)
        both = jnp.where(sub == 0, mean[i:i + 1, :], jnp.where(sub == 1, rstd[i:i + 1, :], 0.0)).T
        mean_v[r, :] = both[:, 0:1]
        rstd_v[r, :] = both[:, 1:2]
    loads[4].wait()
    loads[8].wait()

    def p_copy(j, d):
        ch = pair_chunk(j, d)
        return pltpu.make_async_remote_copy(
            src_ref=pb.at[ch, pl.ds(pl.multiple_of((1 - core) * PART, 16), PART)], dst_ref=r0.at[ch],
            send_sem=p_send, recv_sem=p_recv.at[j],
            device_id={"dp": sibling}, device_id_type=MESH)

    def at_pos(axis, off):
        if axis == 0:
            return (lax.rem(px + SIDE + off, SIDE) * SIDE + py) * 2 + core
        return (px * SIDE + lax.rem(py + SIDE + off, SIDE)) * 2 + core

    class Tree:
        def __init__(self, j, d, part, stage):
            self.j, self.d, self.stage = j, d, stage
            if part is None:
                self.base, self.size = 0, PART // 2
                self.slots, self.send, self.recv = tree.at[j, d, stage], rs_send.at[j, d], rs_recv.at[j, d, stage]
            else:
                self.size = PART // LAST_PARTS // 2
                self.base = part * 2 * self.size
                self.slots = end_tree.at[d, part, stage]
                self.send, self.recv = end_send.at[d, part], end_recv.at[d, part, stage]
            ch = pair_chunk(j, d)
            self.axis = 1 - d if stage == 0 else d
            place, goal = (px, py), (ch // SIDE, lax.rem(ch, SIDE))
            self.keeps = chip == ch
            self.r = lax.rem(place[self.axis] + SIDE - goal[self.axis], SIDE)
            self.here = place[1 - self.axis] == goal[1 - self.axis] if stage else px >= 0
            self.src = s_v.at[ch] if stage == 0 else t_v.at[j, d]
            self.low = self.r // 2
            self.sgn = 2 * self.low - 1

        def half(self, h):
            return pl.ds(pl.multiple_of(self.base + h * self.size, 16), self.size)

        def copy(self, src, off, slot):
            return pltpu.make_async_remote_copy(
                src_ref=src, dst_ref=self.slots.at[slot], send_sem=self.send, recv_sem=self.recv,
                device_id={"dp": at_pos(self.axis, off)}, device_id_type=MESH)

        def is_far(self):
            return jnp.logical_and(self.here, self.r == 2)

        def is_near(self):
            return jnp.logical_and(self.here, lax.rem(self.r, 2) == 1)

        def is_goal(self):
            return jnp.logical_and(self.here, self.r == 0)

        def far(self):
            return [self.copy(self.src.at[self.half(0)], -1, 0), self.copy(self.src.at[self.half(1)], 1, 0)]

        def raw(self):
            return self.copy(self.src.at[self.half(1 - self.low)], self.sgn, 1 + self.low)

        def total(self):
            return self.copy(self.slots.at[1], self.sgn, 3 * self.low)

        def begin(self):
            @pl.when(self.is_far())
            def _():
                for c in self.far():
                    c.start()

            @pl.when(self.is_near())
            def _():
                self.raw().start()

        def relay(self):
            @pl.when(self.is_near())
            def _():
                self.copy(self.slots.at[0], 1, 0).wait_recv()
                self.slots[1] = (self.slots[0].astype(F32) + self.src[self.half(self.low), :].astype(F32)).astype(BF16)
                self.total().start()

        def finish(self):
            @pl.when(self.is_goal())
            def _():
                pltpu.make_async_copy(self.slots, self.slots, self.recv).wait()
                for h in range(2):
                    lo = self.base + h * self.size
                    rows = slice(lo, lo + self.size)
                    res = (
                        self.src[rows, :].astype(F32) + self.slots[h].astype(F32) + self.slots[2 + h].astype(F32))
                    if self.stage == 0:
                        t_v[self.j, self.d, rows, :] = res.astype(BF16)
                    else:
                        g_out[rows, :] = res

        def drain(self):
            @pl.when(jnp.logical_not(self.keeps))
            def _():
                sent = self.slots.at[pl.ds(0, 2)]
                pltpu.make_async_copy(sent, sent, self.send).wait()

    def parts_of(j):
        return range(LAST_PARTS) if isinstance(j, int) and j == NZ - 1 else (None,)

    def trees(j, stage, parts=None):
        return [Tree(j, d, part, stage) for part in parts or parts_of(j) for d in range(2)]

    def combine(j):
        two = r0.at[pl.ds(0, 2)]
        pltpu.make_async_copy(two, two, p_recv.at[j]).wait()
        for d in range(2):
            ch = pair_chunk(j, d)
            mine = pb[ch, pl.ds(pl.multiple_of(core * PART, 16), PART), :].astype(F32)
            s_v[ch] = (mine + r0[ch].astype(F32)).astype(BF16)
        for t in trees(j, 0):
            t.begin()

    def second(j):
        for part in parts_of(j):
            for t in trees(j, 0, (part,)):
                t.finish()
            for t in trees(j, 1, (part,)):
                t.begin()

    def relay(j, stage):
        for t in trees(j, stage):
            t.relay()

    def last(j):
        for t in trees(j, 1):
            t.finish()

    def process(j):
        for d in range(2):
            ch = pair_chunk(j, d)

            def norm_tile(i, c):
                r = pl.ds(pl.multiple_of(i * TILE, TILE), TILE)
                gain = gain_ref[:, pl.ds(pl.multiple_of(ch * WIDTH, HD), WIDTH)]
                xs = xg[ch, r, :].astype(F32)
                n_v[d, r, :] = ((xs - mean_v[r, :]) * rstd_v[r, :] * gain).astype(BF16)
                return c

            lax.fori_loop(0, ROWS // TILE, norm_tile, 0, unroll=True)
            pb[ch] = dot(n_v[d], vr_b[...], 0, 0).astype(BF16)
            if d == 1:
                p_copy(j, 0).start()
        p_copy(j, 1).start()
        for d in range(2):
            ch = pair_chunk(j, d)
            vacc[...] += dot(n_v[d], w_v[pl.ds(pl.multiple_of(ch * WIDTH, HD), WIDTH), :], 1, 0)

    def early(j, carry):
        @pl.when(j >= 3)
        def _():
            arrival(j)

        process(j)

        @pl.when(j >= 1)
        def _():
            combine(j - 1)

        @pl.when(j >= 2)
        def _():
            relay(j - 2, 0)

        @pl.when(j >= 3)
        def _():
            second(j - 3)

        return carry

    lax.fori_loop(0, 4, early, 0)

    arrival(4)
    combine(3)
    relay(2, 0)
    second(1)
    process(4)
    combine(4)
    relay(0, 1)
    relay(3, 0)
    second(2)
    relay(1, 1)
    arrival(5)
    relay(4, 0)
    second(3)
    relay(2, 1)
    last(0)
    last(1)
    process(5)
    combine(5)
    second(4)
    relay(3, 1)
    last(2)
    arrival(6)
    relay(5, 0)
    relay(4, 1)
    process(6)
    combine(6)
    second(5)
    last(3)
    last(4)
    arrival(7)
    relay(6, 0)
    relay(5, 1)
    process(7)

    def backward(h):
        cols = slice(h * HD, (h + 1) * HD)
        for t in range(tiles):
            r = slice(t * TILE, (t + 1) * TILE)
            lo = min(max(t * TILE - 64, 0), ROWS - SPAN)
            win = slice(lo, lo + SPAN)
            p = wts[h * tiles + t]
            dp_t = dot(vr_b[win, cols], cot_v[r, cols], 1, 1)
            centre = jnp.sum(p * dp_t, axis=0, keepdims=True)
            ds = (p * (dp_t - centre)).astype(BF16)
            dk_f[win, cols] += dot(ds, q_v[r, cols], 1, 0)
            dq_out[r, cols] = (dot(ds, k_v[win, cols], 0, 0) * scale).astype(BF16)

    vr_b[...] = vacc[...].astype(BF16)
    dk_f[...] = jnp.zeros_like(dk_f)
    combine(NZ - 1)
    second(NZ - 2)
    relay(NZ - 1, 0)
    last(NZ - 3)
    relay(NZ - 2, 1)
    backward(0)
    backward(1)
    second(NZ - 1)
    relay(NZ - 1, 1)
    last(NZ - 2)
    backward(2)
    dk_out[...] = (dk_f[...] * scale).astype(BF16)
    stores = [
        pltpu.make_async_copy(dq_out, dq_hbm, local_sem.at[0]),
        pltpu.make_async_copy(dk_out, dk_hbm, local_sem.at[1]),
        pltpu.make_async_copy(g_out, g_hbm, local_sem.at[2]),
    ]
    stores[0].start()
    stores[1].start()

    def drain(j, carry):
        for t in trees(j, 0):
            t.drain()
        return carry

    lax.fori_loop(0, NZ - 1, drain, 0)
    pltpu.make_async_copy(r0, r0, p_send).wait()
    last(NZ - 1)
    stores[2].start()
    drain(NZ - 1, 0)
    sent = xg.at[pl.ds(0, 2 * (NZ - 1))]
    pltpu.make_async_copy(sent, sent, ag_send).wait()
    pltpu.make_async_copy(some, some, cot_send).wait()
    pltpu.make_async_copy(first, first, st_send).wait()
    for store in stores:
        store.wait()


def hand_over(g_in, dq_in, dk_in, g_hbm, dq_hbm, dk_hbm, sem):
    copies = [
        pltpu.make_async_copy(a, o, sem.at[i])
        for i, (a, o) in enumerate(((g_in, g_hbm), (dq_in, dq_hbm), (dk_in, dk_hbm)))
    ]
    for c in copies:
        c.start()
    for c in copies:
        c.wait()


def body(
    patches, norm_gain, value_weight, queries, key_vectors, head_cotangent, image_owner, patch_count
):
    any_ = pl.BlockSpec(memory_space=pl.ANY)
    V, DMA = pltpu.VMEM, pltpu.SemaphoreType.DMA
    shapes = tuple(
        jax.ShapeDtypeStruct(shape, kind)
        for shape, kind in (((PART, WIDTH), F32), ((ROWS, WIDTH), BF16), ((ROWS, WIDTH), BF16)))
    done = pl.pallas_call(
        kernel,
        out_shape=shapes,
        in_specs=[any_] * 8,
        out_specs=(any_,) * 3,
        scratch_shapes=[
            V((1, NZ * 2 * WIDTH), F32),
            V((NDP, NDP), jnp.int32),
            V((NDP, NDP), jnp.int32),
            V((PART, WIDTH), F32),
            V((ROWS, WIDTH), BF16),
            V((ROWS, WIDTH), BF16),
            V((CHIPS, ROWS, WIDTH), BF16),
            V((NZ * 2 * WIDTH, WIDTH), BF16),
            V((ROWS, WIDTH), BF16),
            V((ROWS, WIDTH), BF16),
            V((NDP * CAP, WIDTH), BF16),
            V((ROWS, WIDTH), BF16),
            V((8, TILE), F32),
            V((NZ, 8, TILE), F32),
            V((ROWS, 1), F32),
            V((ROWS, 1), F32),
            V((ROWS, 1), F32),
            V((ROWS, 1), F32),
            V((8, ROWS), F32),
            V((3 * ROWS // TILE, SPAN, TILE), F32),
            V((ROWS, WIDTH), F32),
            V((ROWS, WIDTH), BF16),
            V((ROWS, WIDTH), F32),
            V((2, ROWS, WIDTH), BF16),
            V((CHIPS, 2 * PART, WIDTH), BF16),
            V((CHIPS, PART, WIDTH), BF16),
            V((CHIPS, PART, WIDTH), BF16),
            V((ROWS, WIDTH), F32),
            V((NZ, 2, PART, WIDTH), BF16),
            V((NZ - 1, 2, 2, 4, PART // 2, WIDTH), BF16),
            DMA((9,)), DMA, DMA((2, 7)), DMA, DMA, DMA, DMA, DMA, DMA((NZ,)),
            DMA((NZ - 1, 2)), DMA((NZ - 1, 2, 2)),
            V((2, LAST_PARTS, 2, 4, PART // LAST_PARTS // 2, WIDTH), BF16),
            DMA((2, LAST_PARTS)), DMA((2, LAST_PARTS, 2)),
        ],
        compiler_params=pltpu.CompilerParams(
            collective_id=0, has_side_effects=True, vmem_limit_bytes=50 * 1024 * 1024
        ),
    )(
        *(
            pltpu.with_memory_space_constraint(a, pltpu.HBM)
            for a in (
                patches, norm_gain.reshape(1, -1), value_weight, queries, key_vectors, head_cotangent,
                image_owner, patch_count,
            )
        )
    )
    return pl.pallas_call(
        hand_over,
        out_shape=shapes,
        in_specs=[pl.BlockSpec(memory_space=pltpu.VMEM)] * 3,
        out_specs=(any_,) * 3,
        scratch_shapes=[DMA((3,))],
        compiler_params=pltpu.CompilerParams(vmem_limit_bytes=4 * 1024 * 1024),
    )(*done)


def solution(mesh):
    return jax.shard_map(
        body,
        mesh=mesh,
        in_specs=(
            P("dp", "mp"), P(), P(None, "mp"), P("dp", "mp"), P("dp", "mp"), P("dp", "mp"), P(), P(),
        ),
        out_specs=(P("dp", "mp"), P("dp", "mp"), P("dp", "mp")),
        check_vma=False,
    )
```
